256 devices in a mesh: view: 16 (over y, x), scene: 16 (over z, core).
Axes of the slice: x: 4, y: 4, z: 8, core: 2. Of those that a mesh axis runs over, the one named last changes fastest.
Arguments:
- params: float32 [14, 262144], P(None, 'scene'), may hold values from -3 to 3
- pixel_basis: float32 [512, 13, 256], P('view'), may hold values from -6 to 6
- tile_blocks: int32 [512, 16, 2], P('view', 'scene'), may hold values from 0 to 127
- depth_rank: int32 [512, 32], P('view'), may hold values from 0 to 31, each once within a row
- target: float32 [512, 256], P('view'), may hold values from -0.3 to 0.3
Outputs:
- step: float32 [14, 262144], P(None, 'scene')
- residual: float32 [512, 256], P('view')
The draws below stay inside these ranges and needn't reach their ends.
Inputs may be any that keep to these rules, and one draw needn't show every extreme that they name: `tile_blocks`: index of a block among the 128 blocks held by the owner named by the second dimension; a tile may list a block more than once. `depth_rank`: each row is a permutation of the 32 slots; a lower rank lies in front.
All inputs are finite; a program needn't handle non-finite values.
Results may differ from the reference program's by a relative error of at most 0.0003.
Values sent between devices are 32-bit elements; how exact they have to be, the bound alone decides.
A program may use at most 128 MiB of HBM per device.

```python
import math
import jax
import jax.numpy as jnp
import numpy as np
from jax import lax

PARAMS = 14
BLOCK_SIZE = 128
TILE_PIXELS = 256
SLOTS_OWNER = 2
ITERS = 3
LOCAL_BLOCKS = 128
GAUSSIANS = 262144
SLOTS = 32
TILES = 512
N_SCENE = 16


def with_ends(entries, own_key, low, largest):
    longest = entries.shape.index(max(entries.shape))
    spots = []
    for shift in (0, 1):
        where = [jax.random.randint(jax.random.fold_in(own_key, axis), (), 0, length) for axis, length in enumerate(entries.shape)]
        where[longest] = (where[longest] + shift) % entries.shape[longest]
        spots.append(tuple(where))
    return entries.at[spots[0]].set(low).at[spots[1]].set(largest)


def block_levels(own_key, extent, cuts, least, high):
    gain = 1.0
    for axis_at, blocks in cuts:
        draws = jax.random.uniform(jax.random.fold_in(jax.random.fold_in(own_key, 6), axis_at), (blocks,), jnp.float32, least / len(cuts), high / len(cuts))
        gain = gain * jnp.repeat(jnp.exp(draws), extent[axis_at] // blocks).reshape((-1,) + (1,) * (len(extent) - 1 - axis_at))
    return gain


def cumulative_ranks(number_of, lean):
    weights = [(1 << 20) // math.isqrt(grade ** lean) + 1 for grade in range(1, number_of + 1)]
    scale = 1 + sum(weights) // (1 << 30)
    return np.cumsum(np.array([max(1, weight // scale) for weight in weights]))


def ranked(own_key, extent, amount, slope):
    table = cumulative_ranks(amount, slope)
    ticket = jax.random.randint(jax.random.fold_in(own_key, 1), extent, 0, int(table[amount - 1]))
    rank = jnp.searchsorted(jnp.asarray(table, jnp.int32), ticket, side="right")
    return jax.random.permutation(jax.random.fold_in(own_key, 2), amount)[rank].astype(jnp.int32)


def noise(rng, dims, scale, most, split=(), held_as=jnp.bfloat16):
    array = scale * jax.random.normal(rng, dims, jnp.float32)
    if split:
        array = array * block_levels(rng, dims, split, -0.22, 0.18)
    return jnp.clip(array, -most, most).astype(held_as)


def setup_inputs(seed: int = 0) -> dict:
    key_list = jax.random.split(jax.random.key(seed), 6)
    return {
        "params": noise(key_list[0], (PARAMS, GAUSSIANS), 0.5, 3.0, ((1, 16),), jnp.float32),
        "pixel_basis": noise(key_list[1], (TILES, PARAMS - 1, TILE_PIXELS), 1.0, 6.0, ((0, 16),), jnp.float32),
        "tile_blocks": with_ends(ranked(key_list[2], (TILES, N_SCENE, SLOTS_OWNER), LOCAL_BLOCKS, 2), jax.random.fold_in(key_list[2], 3), 0, LOCAL_BLOCKS - 1).astype(jnp.int32),
        "depth_rank": jax.vmap(lambda own: jax.random.permutation(own, SLOTS))(jax.random.split(key_list[3], TILES)).reshape((TILES, SLOTS)).astype(jnp.int32),
        "target": noise(key_list[4], (TILES, TILE_PIXELS), 0.05, 0.3, ((0, 16),), jnp.float32),
    }


alpha_max = 0.004
damping = 0.1
ridge_term = 0.0001
highest = lax.Precision.HIGHEST


def tile_factors(param_blocks, basis_tile, ids_tile, rank_tile):
    param_count = param_blocks.shape[0]
    pieces = jnp.take(param_blocks, ids_tile, axis=1)
    logits = jnp.einsum('cq,ckg->kqg', basis_tile, pieces[:param_count - 1], precision=highest)
    opacity = alpha_max * jax.nn.sigmoid(logits)
    log_keep = jnp.log1p(-opacity)
    inner_log = jnp.cumsum(log_keep, axis=2) - log_keep
    block_log = jnp.sum(log_keep, axis=2)
    earlier = (rank_tile[None, :] < rank_tile[:, None]).astype(jnp.float32)
    front_log = jnp.dot(earlier, block_log, precision=highest)
    weight = jnp.exp(front_log[:, :, None] + inner_log) * opacity
    colour = pieces[param_count - 1][:, None, :]
    slopes = weight * colour * (1.0 - opacity / alpha_max)
    return weight, slopes, colour


def reference(params, pixel_basis, tile_blocks, depth_rank, target):
    param_count = params.shape[0]
    param_blocks = params.reshape(param_count, params.shape[1] // BLOCK_SIZE, BLOCK_SIZE)
    offsets = jnp.arange(N_SCENE, dtype=jnp.int32) * LOCAL_BLOCKS
    global_ids = (tile_blocks + offsets[None, :, None]).reshape(TILES, SLOTS).astype(jnp.int32)
    tile_inputs = (pixel_basis, global_ids, depth_rank)

    def render_tile(inputs):
        basis_tile, ids_tile, rank_tile = inputs
        weight, slopes, colour = tile_factors(param_blocks, basis_tile, ids_tile, rank_tile)
        return jnp.sum(weight * colour, axis=(0, 2))

    residual = lax.map(render_tile, tile_inputs) - target

    def forward(vector):
        def one_tile(inputs):
            basis_tile, ids_tile, rank_tile = inputs
            weight, slopes, colour = tile_factors(param_blocks, basis_tile, ids_tile, rank_tile)
            pieces = jnp.take(vector, ids_tile, axis=1)
            projected = jnp.einsum('cq,ckg->kqg', basis_tile, pieces[:param_count - 1], precision=highest)
            return jnp.sum(slopes * projected + weight * pieces[param_count - 1][:, None, :], axis=(0, 2))

        return lax.map(one_tile, tile_inputs)

    def backward(pixel_vec, squared):
        def one_tile(total, inputs):
            basis_tile, ids_tile, rank_tile, values = inputs
            weight, slopes, colour = tile_factors(param_blocks, basis_tile, ids_tile, rank_tile)
            if squared:
                feature = jnp.einsum('cq,kqg->ckg', basis_tile * basis_tile, slopes * slopes, precision=highest)
                colour_term = jnp.sum(weight * weight, axis=1)
            else:
                feature = jnp.einsum('cq,kqg->ckg', basis_tile, slopes * values[None, :, None], precision=highest)
                colour_term = jnp.sum(weight * values[None, :, None], axis=1)
            stacked = jnp.concatenate([feature, colour_term[None]], axis=0)
            return total.at[:, ids_tile].add(stacked), None

        total, unused = lax.scan(one_tile, jnp.zeros_like(param_blocks), tile_inputs + (pixel_vec,))
        return total

    gradient = backward(residual, False)
    curv_diag = backward(residual, True)
    precondition = (1.0 + damping) * curv_diag + ridge_term

    def apply_system(direction):
        return backward(forward(direction), False) + (damping * curv_diag + ridge_term) * direction

    solution = jnp.zeros_like(gradient)
    remainder = -gradient
    scaled = remainder / precondition
    direction = scaled
    rho_now = jnp.sum(remainder * scaled)
    for iteration in range(ITERS):
        image_dir = apply_system(direction)
        step_size = rho_now / jnp.sum(direction * image_dir)
        solution = solution + step_size * direction
        remainder = remainder - step_size * image_dir
        scaled = remainder / precondition
        rho_next = jnp.sum(remainder * scaled)
        direction = scaled + (rho_next / rho_now) * direction
        rho_now = rho_next
    return solution.reshape(param_count, params.shape[1]), residual
```

```python
import functools

import jax
import jax.numpy as jnp
from jax import lax
from jax.experimental import pallas as pl
from jax.experimental.pallas import tpu as pltpu
from jax.sharding import PartitionSpec as P

MESH = pl.DeviceIdType.MESH
ALPHA = 0.004
DAMPING = 0.1
RIDGE = 0.0001
ITERS = 3
G = 128
CP = 16
f32 = jnp.float32
bf16 = jnp.bfloat16
NT = (((1,), (1,)), ((), ()))
TN = (((0,), (0,)), ((), ()))


def split2(x):
    hi = x.astype(bf16)
    return hi, (x - hi.astype(f32)).astype(bf16)


def split3(x):
    hi = x.astype(bf16)
    rest = x - hi.astype(f32)
    mid = rest.astype(bf16)
    return hi, mid, (rest - mid.astype(f32)).astype(bf16)


def dot(a, b, dims=(((1,), (0,)), ((), ()))):
    return lax.dot_general(a, b, dims, preferred_element_type=f32)


def lanes(ref, row):
    return jnp.concatenate([ref[pl.ds(row, 1), :], ref[pl.ds(row + 1, 1), :]], axis=1)


def kernel(
    n, params, tiles,
    par, basis, ids, ids_rows, rank, target,
    step, residual,
    b16, bst, S, W, hi, lo, stk, onehot,
    bl_out, bl_in, fr_out, fr_in,
    u_out, u_in, s_out, u_all, u_now,
    w_out, rs_in, z, direction, total_step, z_flat, z_shard, shard,
    dot_out, dot_in,
    send_sem, recv_sem,
):
    view = lax.axis_index("view")
    scene = lax.axis_index("scene")
    barrier = pltpu.get_barrier_semaphore()

    def greet(d, c):
        pl.semaphore_signal(barrier, inc=1, device_id=(lax.rem(view + d, n), scene), device_id_type=MESH)
        pl.semaphore_signal(barrier, inc=1, device_id=(view, lax.rem(scene + d, n)), device_id_type=MESH)
        return c

    lax.fori_loop(1, n, greet, 0)


    def send(axis, phase, src_of, dst):
        def body(d, c):
            if axis == "view":
                peer = lax.rem(view + d, n)
                where = (peer, scene)
            else:
                peer = lax.rem(scene + d, n)
                where = (view, peer)
            pltpu.make_async_remote_copy(
                src_ref=src_of(peer), dst_ref=dst, send_sem=send_sem.at[phase], recv_sem=recv_sem.at[phase],
                device_id=where, device_id_type=MESH,
            ).start()
            return c

        lax.fori_loop(1, n, body, 0)

    def wait(phase, received, sent=None):
        sent = received if sent is None else sent
        pltpu.make_async_copy(received, received, recv_sem.at[phase]).wait()
        pltpu.make_async_copy(sent, sent, send_sem.at[phase]).wait()

    block_at = lax.broadcasted_iota(jnp.int32, (G, tiles), 0)
    hot = [jnp.where(block_at == ids_rows[pl.ds(j, 1), :], 1.0, 0.0).astype(bf16) for j in range(2)]
    onehot[...] = jnp.concatenate(hot + hot, axis=1)
    below = lax.broadcasted_iota(jnp.int32, (G, G), 1) < lax.broadcasted_iota(jnp.int32, (G, G), 0)
    below = jnp.where(below, 1.0, 0.0).astype(bf16)
    below = jnp.concatenate([below, below], axis=1)

    halves = [w_out.at[h].reshape(CP * G, G) for h in range(2)]
    for h in range(2):
        halves[h][pl.ds(0, (params - 1) * tiles)] = basis[:, G * h : G * (h + 1)]

    def prepare(t, c):
        full = jnp.concatenate([half[pl.ds(t, params - 1, stride=tiles), :] for half in halves], axis=1)
        full = jnp.concatenate([full, jnp.zeros((CP - params + 1, full.shape[1]), f32)], axis=0)
        b16[t] = full
        bh, bl = split2(full)
        bst[t] = jnp.concatenate([bh, bh, bl], axis=0)
        return c

    lax.fori_loop(0, tiles, prepare, 0)

    def stage(b, c):
        piece = par[:, pl.ds(pl.multiple_of(b * G, G), G)]
        direction[b] = jnp.concatenate([piece, jnp.zeros((CP - params, G), f32)], axis=0)
        return c

    lax.fori_loop(0, G, stage, 0, unroll=4)
    z_flat[8 * (params + 1) :] = jnp.zeros((8 * (CP - params - 1), G), f32)

    def listing_params(t, j):
        return direction[ids[j, t]]

    def slot_row(t, j):
        return 8 * (t // 2) + 4 * j + 2 * lax.rem(t, 2)

    def opacities(t, c):
        bh, bm, bl = split3(b16[t])
        rhs = jnp.concatenate([bh, bm, bh, bl, bh, bm], axis=0)
        for j in range(2):
            p = 2 * t + j
            vh, vm, vl = split3(listing_params(t, j))
            lhs = jnp.concatenate([vh, vh, vm, vh, vl, vm], axis=0)
            logit = dot(lhs, rhs, TN)
            o = ALPHA * (1.0 / (1.0 + jnp.exp(-logit)))
            keep = -o * (1.0 + o * (0.5 + o * (1.0 / 3.0 + o * 0.25)))
            W[p] = o
            kh, kl = split2(keep)
            hi[p, :, :256] = kh
            lo[p, :, :256] = kl
            total = jnp.sum(keep, axis=0, keepdims=True)
            r = slot_row(t, j)
            bl_out[pl.ds(r, 1), :] = total[:, :G]
            bl_out[pl.ds(r + 1, 1), :] = total[:, G:]
        return c

    lax.fori_loop(0, tiles, opacities, 0, unroll=2)

    pl.semaphore_wait(barrier, 2 * (n - 1))
    rows8 = lambda ref, i: ref.at[pl.ds(pl.multiple_of(i * 8, 8), 8)]
    some8 = lambda ref: ref.at[pl.ds(0, 8 * (n - 1))]
    send("scene", 0, lambda peer: rows8(bl_out, peer), rows8(bl_in, scene))
    rows8(bl_in, scene)[...] = rows8(bl_out, scene)[...]

    def weights(t, c):
        for j in range(2):
            p = 2 * t + j
            keeps = jnp.concatenate([hi[p, :, :256], lo[p, :, :256]], axis=0)
            inner = dot(below, keeps)
            o = W[p]
            colour = jnp.transpose(listing_params(t, j))[:, params - 1 : params]
            w = jnp.exp(inner) * o
            W[p] = w
            S[p] = w * colour * (1.0 - o * (1.0 / ALPHA))
        return c

    lax.fori_loop(0, tiles // 2, weights, 0)

    wait(0, some8(bl_in), some8(bl_out))
    slots = 2 * n
    eye = lax.broadcasted_iota(jnp.int32, (slots, slots), 0) == lax.broadcasted_iota(jnp.int32, (slots, slots), 1)
    for i in range(2):
        rank_row = jnp.broadcast_to(rank[pl.ds(2 * scene + i, 1), :].astype(f32), (slots, slots))
        rank_col = jnp.sum(jnp.where(eye, rank_row, 0.0), axis=1, keepdims=True)
        earlier = jnp.where(rank_row < rank_col, 1.0, 0.0).astype(bf16)
        for h in range(2):
            lh, lm, ll = split3(bl_in[pl.ds(2 * i + h, slots, stride=4), :])
            front = dot(earlier, lh) + dot(earlier, lm) + dot(earlier, ll)
            fr_out[pl.ds(2 * i + h, slots, stride=4), :] = jnp.exp(front)
    send("scene", 1, lambda peer: rows8(fr_out, peer), rows8(fr_in, scene))
    rows8(fr_in, scene)[...] = rows8(fr_out, scene)[...]

    lax.fori_loop(tiles // 2, tiles, weights, 0)
    wait(1, some8(fr_in), some8(fr_out))

    def u_row(t):
        return 8 * (t // 2) + 2 * lax.rem(t, 2)

    def put_u(t, value):
        r = u_row(t)
        u_out[pl.ds(r, 1), :] = value[:, :G]
        u_out[pl.ds(r + 1, 1), :] = value[:, G:]

    def finish(t, c):
        total = jnp.zeros((1, 2 * G), f32)
        for j in range(2):
            p = 2 * t + j
            factor = lanes(fr_in, slot_row(t, j))
            w = W[p] * factor
            s = S[p] * factor
            W[p] = w
            S[p] = s
            sh, sl = split2(s)
            wh, wl = split2(w)
            hi[p, :, :256] = sh
            hi[p, :, 256:] = wh
            lo[p, :, :256] = sl
            lo[p, :, 256:] = wl
            colour = jnp.transpose(listing_params(t, j))[:, params - 1 : params]
            total = total + jnp.sum(w * colour, axis=0, keepdims=True)
        put_u(t, total)
        return c

    u_out[...] = jnp.zeros_like(u_out)
    lax.fori_loop(0, tiles, finish, 0, unroll=2)

    def scene_scatter(phase, k):
        rows = u_in.at[k]
        send("scene", phase, lambda peer: rows8(u_out, peer), rows8(rows, scene))
        rows8(rows, scene)[...] = rows8(u_out, scene)[...]

    def scene_gather(phase, k):
        wait(phase, some8(u_in.at[k]), some8(u_out))
        total = u_in[k, pl.ds(0, 8), :]
        for i in range(1, n):
            total = total + u_in[k, pl.ds(8 * i, 8), :]
        s_out[...] = total
        send("scene", phase + 1, lambda peer: s_out, rows8(u_all.at[k], scene))
        rows8(u_all.at[k], scene)[...] = total

    def scene_done(phase, k):
        wait(phase + 1, some8(u_all.at[k]))

    def scatter_blocks(slot):
        for c in range(0, params, 2):
            x = jnp.concatenate([stk[pl.ds((c + e) * 2 * tiles, 2 * tiles), :] for e in range(2)], axis=1)
            xh, xl = split2(x)
            out = dot(onehot[...], jnp.concatenate([xh, xl], axis=0))
            w_out[slot, c] = out[:, :G]
            w_out[slot, c + 1] = out[:, G:]

    def put_listing(t, value):
        for j in range(2):
            stk[pl.ds(tiles * j + t, CP, stride=2 * tiles), :] = value[:, G * j : G * (j + 1)]

    blocks8 = lambda ref, i: ref.at[:, pl.ds(pl.multiple_of(i * 8, 8), 8), :]
    most_blocks = lambda ref: ref.at[:, pl.ds(0, 8 * (n - 1)), :]

    def view_scatter(phase, slot, k):
        out = w_out.at[slot, pl.ds(0, params + 1)]
        send("view", phase, lambda peer: blocks8(out, peer), rs_in.at[k, view])
        rs_in[k, view] = w_out[slot, pl.ds(0, params + 1), pl.ds(pl.multiple_of(view * 8, 8), 8), :]

    def view_total(phase, slot, k):
        wait(phase, rs_in.at[k, pl.ds(0, n - 1)], most_blocks(w_out.at[slot, pl.ds(0, params + 1)]))
        return lax.fori_loop(1, n, lambda i, a: a + rs_in[k, i], rs_in[k, 0])

    is_colour = lax.broadcasted_iota(jnp.int32, (CP, 256), 0) == params - 1

    def transpose_rows(left_s, left_w, right_hi, right_lo):
        sh, sl = split2(left_s)
        wh, wl = split2(left_w)
        high = jnp.concatenate([sh, wh], axis=1)
        both = jnp.concatenate([high, jnp.concatenate([sl, wl], axis=1)], axis=0)
        first = dot(both, right_hi, NT)
        return first[:CP] + first[CP:] + dot(high, right_lo, NT)

    scene_scatter(2, 0)

    def diagonal(t, c):
        left_s = b16[t] * b16[t]
        left_w = jnp.where(is_colour, 1.0, 0.0)
        parts = []
        for j in range(2):
            p = 2 * t + j
            sh, sl = split2(S[p] * S[p])
            wh, wl = split2(W[p] * W[p])
            parts.append(transpose_rows(
                left_s, left_w, jnp.concatenate([sh, wh], axis=1), jnp.concatenate([sl, wl], axis=1)))
        put_listing(t, jnp.concatenate(parts, axis=1))
        return c

    lax.fori_loop(0, tiles // 2, diagonal, 0, unroll=2)
    scene_gather(2, 0)
    lax.fori_loop(tiles // 2, tiles, diagonal, 0, unroll=2)
    scatter_blocks(0)
    w_out[0, params] = jnp.zeros((G, G), f32)
    view_scatter(4, 0, 0)
    scene_done(2, 0)

    def apply_transpose(t, u):
        left_s = b16[t] * u
        left_w = jnp.where(is_colour, u, 0.0)
        right_hi = jnp.concatenate([hi[2 * t], hi[2 * t + 1]], axis=0)
        right_lo = jnp.concatenate([lo[2 * t], lo[2 * t + 1]], axis=0)
        put_listing(t, transpose_rows(left_s, left_w, right_hi, right_lo))

    def gradient(t, c):
        u = lanes(u_all.at[0], u_row(t)) - target[pl.ds(t, 1), :]
        residual[pl.ds(t, 1), :] = u
        apply_transpose(t, u)
        return c

    lax.fori_loop(0, tiles, gradient, 0, unroll=4)
    scatter_blocks(1)
    w_out[1, params] = jnp.zeros((G, G), f32)
    view_scatter(5, 1, 1)

    pixel_row = lax.rem(lax.broadcasted_iota(jnp.int32, (8 * n, G), 0), 8) < 4
    R, Z, DP, D = 0, 1, 2, 3

    def lane_sum(x):
        return jnp.sum(x, axis=1, keepdims=True)

    diag = view_total(4, 0, 0)[:params]
    shard[D] = diag
    shard[R] = -view_total(5, 1, 1)[:params]

    def gather_z(k, phase):
        d = shard[D]
        r = shard[R]
        zs = r / ((1.0 + DAMPING) * d + RIDGE)
        dz = (DAMPING * d + RIDGE) * zs
        part = lambda x: jnp.sum(jnp.sum(x, axis=0), axis=0, keepdims=True)
        rows = [part(r * zs), part(zs * dz)]
        rows.append(part(shard[Z] * dz) if k else jnp.zeros((1, G), f32))
        rows.append(jnp.zeros((5, G), f32))
        z_flat[pl.ds(0, 8 * params)] = zs.reshape(8 * params, G)
        z_flat[pl.ds(8 * params, 8)] = jnp.concatenate(rows, axis=0)
        for i in range(8):
            z_shard[k, i] = z_flat[pl.ds(i, CP, stride=8), :]
        send("view", phase, lambda peer: z_shard.at[k], rows8(z.at[k], view))
        rows8(z.at[k], view)[...] = z_shard[k]
        return zs

    one = jnp.ones((1, 1), f32)
    rz_old, pdp = one, 0.0 * one
    phase = 6
    for k in range(ITERS):
        zs = gather_z(k, phase)
        wait(phase, some8(z.at[k]))
        phase += 1
        flat = z.at[k].reshape(CP * G, G)

        def forward(t, c):
            v = jnp.concatenate(
                [z[k, ids[j, t]] for j in range(2)], axis=1)
            vh, vl = split2(v)
            lhs = jnp.concatenate([vh, vl, vh], axis=0)
            total = jnp.zeros((1, 2 * G), f32)
            for j in range(2):
                p = 2 * t + j
                projected = dot(lhs[:, G * j : G * (j + 1)], bst[t], TN)
                tint = jnp.transpose(v[:, G * j : G * (j + 1)])[:, params - 1 : params]
                total = total + jnp.sum(S[p] * projected + W[p] * tint, axis=0, keepdims=True)
            put_u(t, total)
            return c

        lax.fori_loop(0, tiles, forward, 0, unroll=4)
        sums = [
            jnp.sum(flat[pl.ds(CP * i + params, n, stride=8 * CP), :], axis=0, keepdims=True) for i in range(3)]
        sums = jnp.concatenate(sums + [sums[0]], axis=0)
        for i in range(n):
            u_out[pl.ds(8 * i + 4, 4), :] = sums
        scene_scatter(phase, k + 1)
        scene_gather(phase, k + 1)
        scene_done(phase, k + 1)
        phase += 2
        totals = lane_sum(u_all[k + 1, pl.ds(4, 4), :])
        rz, zdz, zdp = totals[0:1], totals[1:2], totals[2:3]
        beta = rz / rz_old if k else 0.0 * one
        u = u_all[k + 1] + beta * u_now[...] if k else u_all[k + 1]
        u = jnp.where(pixel_row, u, 0.0)
        u_now[...] = u
        pdp = zdz + 2.0 * beta * zdp + beta * beta * pdp
        square = jnp.sum(u * u, axis=0, keepdims=True)
        if k:
            direction[...] = z[k] + beta * direction[...]
            shard[Z] = zs + beta * shard[Z]
        else:
            direction[...] = z[k]
            shard[Z] = zs
        if k + 1 < ITERS:
            lax.fori_loop(0, tiles, lambda t, c: (apply_transpose(t, lanes(u_now, u_row(t))), c)[1], 0, unroll=4)
            scatter_blocks(k)
            w_out[k, params] = jnp.broadcast_to(square, (G, G))
            view_scatter(phase, k, k + 2)
            w = view_total(phase, k, k + 2)
            phase += 1
            a = rz / (lane_sum(w[params, 0:1]) + pdp)
            image = w[:params] + (DAMPING * shard[D] + RIDGE) * shard[Z]
            shard[R] = shard[R] - a * image
        else:
            dot_out[...] = jnp.broadcast_to(square, (8, G))
            send("view", phase, lambda peer: dot_out, rows8(dot_in, view))
            rows8(dot_in, view)[...] = dot_out[...]
            wait(phase, some8(dot_in))
            total = dot_in[pl.ds(0, 1), :]
            for i in range(1, n):
                total = total + dot_in[pl.ds(8 * i, 1), :]
            a = rz / (lane_sum(total) + pdp)
        if k + 1 == ITERS:
            for b in range(G):
                step[:, pl.ds(b * G, G)] = (total_step[b] + a * direction[b])[:params]
        elif k:
            total_step[...] = total_step[...] + a * direction[...]
        else:
            total_step[...] = a * direction[...]
        rz_old = rz


def local(n, params, pixel_basis, tile_blocks, depth_rank, target):
    count = params.shape[0]
    tiles, _, pixels = pixel_basis.shape
    ids = tile_blocks.transpose(1, 2, 0).reshape(2, tiles)
    basis = pixel_basis.transpose(1, 0, 2).reshape((count - 1) * tiles, pixels)
    vmem = pl.BlockSpec(memory_space=pltpu.VMEM)
    lists = 2 * tiles
    phases = 6 + 4 * (ITERS - 1) + 4
    return pl.pallas_call(
        functools.partial(kernel, n, count, tiles),
        out_shape=(
            jax.ShapeDtypeStruct((count, G * G), f32),
            jax.ShapeDtypeStruct((tiles, pixels), f32),
        ),
        in_specs=[vmem, vmem, pl.BlockSpec(memory_space=pltpu.SMEM), vmem, vmem, vmem],
        out_specs=(vmem, vmem),
        scratch_shapes=[
            pltpu.VMEM((tiles, CP, pixels), f32),
            pltpu.VMEM((tiles, 3 * CP, pixels), bf16),
            pltpu.VMEM((lists, G, pixels), f32),
            pltpu.VMEM((lists, G, pixels), f32),
            pltpu.VMEM((lists, G, 2 * pixels), bf16),
            pltpu.VMEM((lists, G, 2 * pixels), bf16),
            pltpu.VMEM((CP * lists, G), f32),
            pltpu.VMEM((G, 2 * lists), bf16),
            pltpu.VMEM((8 * n, G), f32),
            pltpu.VMEM((8 * n, G), f32),
            pltpu.VMEM((8 * n, G), f32),
            pltpu.VMEM((8 * n, G), f32),
            pltpu.VMEM((8 * n, G), f32),
            pltpu.VMEM((ITERS + 1, 8 * n, G), f32),
            pltpu.VMEM((8, G), f32),
            pltpu.VMEM((ITERS + 1, 8 * n, G), f32),
            pltpu.VMEM((8 * n, G), f32),
            pltpu.VMEM((2, CP, G, G), f32),
            pltpu.VMEM((ITERS + 1, n, count + 1, 8, G), f32),
            pltpu.VMEM((ITERS, G, CP, G), f32),
            pltpu.VMEM((G, CP, G), f32),
            pltpu.VMEM((G, CP, G), f32),
            pltpu.VMEM((8 * CP, G), f32),
            pltpu.VMEM((ITERS, 8, CP, G), f32),
            pltpu.VMEM((4, count, 8, G), f32),
            pltpu.VMEM((8, G), f32),
            pltpu.VMEM((8 * n, G), f32),
            pltpu.SemaphoreType.DMA((phases,)),
            pltpu.SemaphoreType.DMA((phases,)),
        ],
        compiler_params=pltpu.CompilerParams(
            collective_id=0, has_side_effects=True, vmem_limit_bytes=64 * 1024 * 1024 - 65536),
        name="lm_step",
    )(params, basis, ids, ids, depth_rank, target)


def solution(mesh):
    in_specs = (
        P(None, "scene"),
        P("view", None, None),
        P("view", "scene", None),
        P("view", None),
        P("view", None),
    )
    out_specs = (P(None, "scene"), P("view", None))
    step = functools.partial(local, mesh.shape["scene"])
    return jax.shard_map(step, mesh=mesh, in_specs=in_specs, out_specs=out_specs, check_vma=False)
```

```python
import functools

import jax
import jax.numpy as jnp
from jax import lax
from jax.experimental import pallas as pl
from jax.experimental.pallas import tpu as pltpu
from jax.sharding import PartitionSpec as P

MESH = pl.DeviceIdType.MESH
ALPHA = 0.004
DAMPING = 0.1
RIDGE = 0.0001
ITERS = 3
SIDE = 4
SEMS = 128
G = 128
CP = 16
f32 = jnp.float32
bf16 = jnp.bfloat16
NT = (((1,), (1,)), ((), ()))
TN = (((0,), (0,)), ((), ()))


def split2(x):
    hi = x.astype(bf16)
    return hi, (x - hi.astype(f32)).astype(bf16)


def split3(x):
    hi = x.astype(bf16)
    rest = x - hi.astype(f32)
    mid = rest.astype(bf16)
    return hi, mid, (rest - mid.astype(f32)).astype(bf16)


def dot(a, b, dims=(((1,), (0,)), ((), ()))):
    return lax.dot_general(a, b, dims, preferred_element_type=f32)


def lanes(ref, row):
    return jnp.concatenate([ref[pl.ds(row, 1), :], ref[pl.ds(row + 1, 1), :]], axis=1)


def kernel(
    n, params, tiles,
    par, basis, ids, ids_rows, rank, target,
    step, residual,
    b16, bst, S, W, hi, lo, stk, onehot,
    bl_out, bl_in, fr_out, fr_in,
    u_out, u_pair, u_z, u_now, tally_out, tally_in,
    w_out, part_a, part_b, half_a, half_b, last_a, last_b,
    z, direction, total_step, z_flat, z_shard, shard, dot_in,
    sems,
):
    view = lax.axis_index("view")
    scene = lax.axis_index("scene")
    y, x = view // SIDE, lax.rem(view, SIDE)
    zz, core = scene // 2, lax.rem(scene, 2)
    partner = (view, scene + 1 - 2 * core)
    barrier = pltpu.get_barrier_semaphore()

    def greet(d, c):
        pl.semaphore_signal(barrier, inc=1, device_id=(lax.rem(view + d, n), scene), device_id_type=MESH)
        pl.semaphore_signal(barrier, inc=1, device_id=(lax.rem(view + d, n), scene + 1 - 2 * core), device_id_type=MESH)
        pl.semaphore_signal(barrier, inc=1, device_id=(view, lax.rem(scene + d, n)), device_id_type=MESH)
        return c

    lax.fori_loop(1, n, greet, 0)
    counter = iter(range(SEMS))
    new_sem = lambda: sems.at[next(counter)]

    def push(src, dst, send_sem, recv_sem, where):
        pltpu.make_async_remote_copy(
            src_ref=src, dst_ref=dst, send_sem=send_sem, recv_sem=recv_sem, device_id=where, device_id_type=MESH,
        ).start()

    def wait(ref, sem):
        pltpu.make_async_copy(ref, ref, sem).wait()

    def to_scene(src_of, dst, send_sem, recv_sem):
        def body(d, c):
            peer = lax.rem(scene + d, n)
            push(src_of(peer), dst, send_sem, recv_sem, (view, peer))
            return c

        lax.fori_loop(1, n, body, 0)

    block_at = lax.broadcasted_iota(jnp.int32, (G, tiles), 0)
    hot = [jnp.where(block_at == ids_rows[pl.ds(j, 1), :], 1.0, 0.0).astype(bf16) for j in range(2)]
    onehot[...] = jnp.concatenate(hot + hot, axis=1)
    below = lax.broadcasted_iota(jnp.int32, (G, G), 1) < lax.broadcasted_iota(jnp.int32, (G, G), 0)
    below = jnp.where(below, 1.0, 0.0).astype(bf16)
    below = jnp.concatenate([below, below], axis=1)

    halves = [w_out.at[h].reshape(n * (params + 1) * 8, G) for h in range(2)]
    for h in range(2):
        halves[h][pl.ds(0, (params - 1) * tiles)] = basis[:, G * h : G * (h + 1)]

    def prepare(t, c):
        full = jnp.concatenate([half[pl.ds(t, params - 1, stride=tiles), :] for half in halves], axis=1)
        full = jnp.concatenate([full, jnp.zeros((CP - params + 1, full.shape[1]), f32)], axis=0)
        b16[t] = full
        bh, bl = split2(full)
        bst[t] = jnp.concatenate([bh, bh, bl], axis=0)
        return c

    lax.fori_loop(0, tiles, prepare, 0)

    def stage(b, c):
        piece = par[:, pl.ds(pl.multiple_of(b * G, G), G)]
        direction[b] = jnp.concatenate([piece, jnp.zeros((CP - params, G), f32)], axis=0)
        return c

    lax.fori_loop(0, G, stage, 0, unroll=4)
    z_flat[8 * (params + 1) :] = jnp.zeros((8 * (CP - params - 1), G), f32)

    def listing_params(t, j):
        return direction[ids[j, t]]

    def slot_row(t, j):
        return 8 * (t // 2) + 4 * j + 2 * lax.rem(t, 2)

    def opacities(t, c):
        bh, bm, bl = split3(b16[t])
        rhs = jnp.concatenate([bh, bm, bh, bl, bh, bm], axis=0)
        for j in range(2):
            p = 2 * t + j
            vh, vm, vl = split3(listing_params(t, j))
            lhs = jnp.concatenate([vh, vh, vm, vh, vl, vm], axis=0)
            logit = dot(lhs, rhs, TN)
            o = ALPHA * (1.0 / (1.0 + jnp.exp(-logit)))
            keep = -o * (1.0 + o * (0.5 + o * (1.0 / 3.0 + o * 0.25)))
            W[p] = o
            kh, kl = split2(keep)
            hi[p, :, :256] = kh
            lo[p, :, :256] = kl
            total = jnp.sum(keep, axis=0, keepdims=True)
            r = slot_row(t, j)
            bl_out[pl.ds(r, 1), :] = total[:, :G]
            bl_out[pl.ds(r + 1, 1), :] = total[:, G:]
        return c

    lax.fori_loop(0, tiles, opacities, 0, unroll=2)

    pl.semaphore_wait(barrier, 3 * (n - 1))
    rows8 = lambda ref, i: ref.at[pl.ds(pl.multiple_of(i * 8, 8), 8)]
    some8 = lambda ref: ref.at[pl.ds(0, 8 * (n - 1))]
    front_sems = [new_sem() for _ in range(4)]
    to_scene(lambda peer: rows8(bl_out, peer), rows8(bl_in, scene), front_sems[0], front_sems[1])
    rows8(bl_in, scene)[...] = rows8(bl_out, scene)[...]

    def weights(t, c):
        for j in range(2):
            p = 2 * t + j
            keeps = jnp.concatenate([hi[p, :, :256], lo[p, :, :256]], axis=0)
            inner = dot(below, keeps)
            o = W[p]
            colour = jnp.transpose(listing_params(t, j))[:, params - 1 : params]
            w = jnp.exp(inner) * o
            W[p] = w
            S[p] = w * colour * (1.0 - o * (1.0 / ALPHA))
        return c

    lax.fori_loop(0, tiles // 2, weights, 0)

    wait(some8(bl_in), front_sems[1])
    wait(some8(bl_out), front_sems[0])
    slots = 2 * n
    eye = lax.broadcasted_iota(jnp.int32, (slots, slots), 0) == lax.broadcasted_iota(jnp.int32, (slots, slots), 1)
    for i in range(2):
        rank_row = jnp.broadcast_to(rank[pl.ds(2 * scene + i, 1), :].astype(f32), (slots, slots))
        rank_col = jnp.sum(jnp.where(eye, rank_row, 0.0), axis=1, keepdims=True)
        earlier = jnp.where(rank_row < rank_col, 1.0, 0.0).astype(bf16)
        for h in range(2):
            lh, lm, ll = split3(bl_in[pl.ds(2 * i + h, slots, stride=4), :])
            front = dot(earlier, lh) + dot(earlier, lm) + dot(earlier, ll)
            fr_out[pl.ds(2 * i + h, slots, stride=4), :] = jnp.exp(front)
    to_scene(lambda peer: rows8(fr_out, peer), rows8(fr_in, scene), front_sems[2], front_sems[3])
    rows8(fr_in, scene)[...] = rows8(fr_out, scene)[...]

    lax.fori_loop(tiles // 2, tiles, weights, 0)
    wait(some8(fr_in), front_sems[3])
    wait(some8(fr_out), front_sems[2])

    def put_u(t, value):
        u_out[pl.ds(2 * t, 1), :] = value[:, :G]
        u_out[pl.ds(2 * t + 1, 1), :] = value[:, G:]

    mine, other = core * (tiles // 2), (1 - core) * (tiles // 2)

    def half_loop(first, body, unroll):
        def step_of(i, c):
            body(first + i)
            return c

        lax.fori_loop(0, tiles // 2, step_of, 0, unroll=unroll)

    def finish(t):
        total = jnp.zeros((1, 2 * G), f32)
        for j in range(2):
            p = 2 * t + j
            factor = lanes(fr_in, slot_row(t, j))
            w = W[p] * factor
            s = S[p] * factor
            W[p] = w
            S[p] = s
            sh, sl = split2(s)
            wh, wl = split2(w)
            hi[p, :, :256] = sh
            hi[p, :, 256:] = wh
            lo[p, :, :256] = sl
            lo[p, :, 256:] = wl
            colour = jnp.transpose(listing_params(t, j))[:, params - 1 : params]
            total = total + jnp.sum(w * colour, axis=0, keepdims=True)
        put_u(t, total)

    half_rows = lambda ref, first: ref.at[pl.ds(pl.multiple_of(2 * first, 8), tiles)]

    class SceneSum:
        def __init__(self, q):
            self.q, self.sems = q, [new_sem() for _ in range(6)]

        def run(self, body, unroll):
            q, sem = self.q, self.sems
            half_loop(other, body, unroll)
            push(half_rows(u_out, other), u_pair.at[q], sem[0], sem[1], partner)
            half_loop(mine, body, unroll)
            wait(u_pair.at[q], sem[1])
            u_z[q, zz] = half_rows(u_out, mine)[...] + u_pair[q]
            for d in (4, 3, 5, 2, 6, 1, 7):
                push(u_z.at[q, zz], u_z.at[q, zz], sem[2], sem[3], (view, lax.rem(scene + 2 * d, n)))
            wait(u_pair.at[q], sem[0])

        def total(self):
            q, sem = self.q, self.sems
            wait(u_z.at[q, pl.ds(0, n // 2 - 1)], sem[3])
            wait(u_z.at[q, pl.ds(0, n // 2 - 1)], sem[2])
            out = u_z[q, 0]
            for i in range(1, n // 2):
                out = out + u_z[q, i]
            return out

        def publish(self, value):
            q, sem = self.q, self.sems
            rows = half_rows(u_now.at[q], mine)
            rows[...] = value
            push(rows, rows, sem[4], sem[5], partner)

        def rest(self):
            q, sem = self.q, self.sems
            wait(half_rows(u_now.at[q], other), sem[5])
            wait(half_rows(u_now.at[q], other), sem[4])

    render = SceneSum(0)
    render.run(finish, 2)

    def scatter_blocks(slot):
        for c in range(0, params, 2):
            x = jnp.concatenate([stk[pl.ds((c + e) * 2 * tiles, 2 * tiles), :] for e in range(2)], axis=1)
            xh, xl = split2(x)
            out = dot(onehot[...], jnp.concatenate([xh, xl], axis=0))
            w_out[slot, :, c] = out[:, :G].reshape(n, 8, G)
            w_out[slot, :, c + 1] = out[:, G:].reshape(n, 8, G)

    def put_listing(t, value):
        for j in range(2):
            stk[pl.ds(tiles * j + t, CP, stride=2 * tiles), :] = value[:, G * j : G * (j + 1)]

    row_a, row_b = pl.ds(0, 8), pl.ds(8, params - 7)

    class ViewScatter:
        def __init__(self, q, slot):
            self.q, self.slot = q, slot
            self.send_sem, self.last = new_sem(), [new_sem(), new_sem()]
            self.first = [[new_sem() for _ in range(SIDE)] for _ in range(2)]

        def start(self):
            q, slot = self.q, self.slot
            for e in (2, 1, 3, 0):
                for d in (2, 1, 3):
                    to_x, to_y = lax.rem(x + d, SIDE), lax.rem(y + d, SIDE)
                    line_y, line_x = lax.rem(y + e, SIDE), lax.rem(x + e, SIDE)
                    push(w_out.at[slot, line_y * SIDE + to_x, row_a], part_a.at[q, d - 1, line_y],
                         self.send_sem, self.first[0][e], (y * SIDE + to_x, scene))
                    push(w_out.at[slot, to_y * SIDE + line_x, row_b], part_b.at[q, d - 1, line_x],
                         self.send_sem, self.first[1][e], (to_y * SIDE + x, scene))

        def middle(self):
            q, slot = self.q, self.slot
            for e in (2, 1, 3, 0):
                line_y, line_x = lax.rem(y + e, SIDE), lax.rem(x + e, SIDE)
                wait(part_a.at[q, :, line_y], self.first[0][e])
                total = w_out[slot, line_y * SIDE + x, row_a] + part_a[q, 0, line_y]
                half_a[q, line_y] = total + part_a[q, 1, line_y] + part_a[q, 2, line_y]
                if e:
                    push(half_a.at[q, line_y], last_a.at[q, e - 1], self.send_sem, self.last[0], (line_y * SIDE + x, scene))
                wait(part_b.at[q, :, line_x], self.first[1][e])
                total = w_out[slot, y * SIDE + line_x, row_b] + part_b[q, 0, line_x]
                half_b[q, line_x] = total + part_b[q, 1, line_x] + part_b[q, 2, line_x]
                if e:
                    push(half_b.at[q, line_x], last_b.at[q, e - 1], self.send_sem, self.last[1], (y * SIDE + line_x, scene))

        def total(self):
            q, slot = self.q, self.slot
            wait(last_a.at[q], self.last[0])
            wait(last_b.at[q], self.last[1])
            wait(w_out.at[slot, pl.ds(0, n - 1)], self.send_sem)
            out_a, out_b = half_a[q, y], half_b[q, x]
            for d in range(SIDE - 1):
                out_a, out_b = out_a + last_a[q, d], out_b + last_b[q, d]
            return jnp.concatenate([out_a, out_b], axis=0)

    is_colour = lax.broadcasted_iota(jnp.int32, (CP, 256), 0) == params - 1

    def transpose_rows(left_s, left_w, right_hi, right_lo):
        sh, sl = split2(left_s)
        wh, wl = split2(left_w)
        high = jnp.concatenate([sh, wh], axis=1)
        both = jnp.concatenate([high, jnp.concatenate([sl, wl], axis=1)], axis=0)
        first = dot(both, right_hi, NT)
        return first[:CP] + first[CP:] + dot(high, right_lo, NT)

    def diagonal(t, c):
        left_s = b16[t] * b16[t]
        left_w = jnp.where(is_colour, 1.0, 0.0)
        parts = []
        for j in range(2):
            p = 2 * t + j
            sh, sl = split2(S[p] * S[p])
            wh, wl = split2(W[p] * W[p])
            parts.append(transpose_rows(
                left_s, left_w, jnp.concatenate([sh, wh], axis=1), jnp.concatenate([sl, wl], axis=1)))
        put_listing(t, jnp.concatenate(parts, axis=1))
        return c

    lax.fori_loop(0, tiles, diagonal, 0, unroll=2)
    scatter_blocks(0)
    w_out[0, :, params] = jnp.zeros((n, 8, G), f32)
    diag_sum = ViewScatter(0, 0)
    diag_sum.start()
    render.publish(render.total())

    def apply_transpose(t, u):
        left_s = b16[t] * u
        left_w = jnp.where(is_colour, u, 0.0)
        right_hi = jnp.concatenate([hi[2 * t], hi[2 * t + 1]], axis=0)
        right_lo = jnp.concatenate([lo[2 * t], lo[2 * t + 1]], axis=0)
        put_listing(t, transpose_rows(left_s, left_w, right_hi, right_lo))

    def gradient(t):
        u = lanes(u_now.at[0], 2 * t) - target[pl.ds(t, 1), :]
        residual[pl.ds(t, 1), :] = u
        apply_transpose(t, u)

    half_loop(mine, gradient, 4)
    diag_sum.middle()
    render.rest()
    half_loop(other, gradient, 4)
    scatter_blocks(1)
    w_out[1, :, params] = jnp.zeros((n, 8, G), f32)
    grad_sum = ViewScatter(1, 1)
    grad_sum.start()

    R, Z, DP, D = 0, 1, 2, 3

    def lane_sum(x):
        return jnp.sum(x, axis=1, keepdims=True)

    shard[D] = diag_sum.total()[:params]
    grad_sum.middle()
    shard[R] = -grad_sum.total()[:params]

    def gather_z(k):
        d = shard[D]
        r = shard[R]
        zs = r / ((1.0 + DAMPING) * d + RIDGE)
        dz = (DAMPING * d + RIDGE) * zs
        part = lambda x: jnp.sum(jnp.sum(x, axis=0), axis=0, keepdims=True)
        rows = [part(r * zs), part(zs * dz)]
        rows.append(part(shard[Z] * dz) if k else jnp.zeros((1, G), f32))
        rows.append(jnp.zeros((5, G), f32))
        z_flat[pl.ds(0, 8 * params)] = zs.reshape(8 * params, G)
        z_flat[pl.ds(8 * params, 8)] = jnp.concatenate(rows, axis=0)
        for i in range(8):
            z_shard[k, i] = z_flat[pl.ds(i, CP, stride=8), :]
        rows8(z.at[k], view)[...] = z_shard[k]
        rest_sem, send_sem = new_sem(), new_sem()
        sem_a, sem_b = [None] + [new_sem() for _ in range(3)], [None] + [new_sem() for _ in range(3)]
        line = z.at[k]
        part_of = lambda owner, h: line.at[pl.ds(pl.multiple_of(8 * owner + 4 * h, 4), 4)]
        own = [z_shard.at[k, pl.ds(4 * h, 4)] for h in range(2)]
        at_x = lambda d: (y * SIDE + lax.rem(x + d, SIDE), scene)
        at_y = lambda d: (lax.rem(y + d, SIDE) * SIDE + x, scene)
        for d in (1, 3, 2):
            push(own[0], part_of(view, 0), send_sem, sem_a[d], at_x(d))
            push(own[1], part_of(view, 1), send_sem, sem_b[d], at_y(d))
        for d in (1, 3, 2):
            push(own[1], part_of(view, 1), send_sem, rest_sem, at_x(d))
            push(own[0], part_of(view, 0), send_sem, rest_sem, at_y(d))
        for d in (1, 3, 2):
            from_x = y * SIDE + lax.rem(x + SIDE - d, SIDE)
            from_y = lax.rem(y + SIDE - d, SIDE) * SIDE + x
            wait(part_of(from_x, 0), sem_a[d])
            for e in (2, 1, 3):
                push(part_of(from_x, 0), part_of(from_x, 0), send_sem, rest_sem, at_y(e))
            wait(part_of(from_y, 1), sem_b[d])
            for e in (2, 1, 3):
                push(part_of(from_y, 1), part_of(from_y, 1), send_sem, rest_sem, at_x(e))
        wait(line.at[pl.ds(0, 4 * 24)], rest_sem)
        wait(line.at[pl.ds(0, 4 * 30)], send_sem)
        return zs

    one = jnp.ones((1, 1), f32)
    rz_old, pdp = one, 0.0 * one
    for k in range(ITERS):
        zs = gather_z(k)
        flat = z.at[k].reshape(CP * G, G)
        sums = [
            jnp.sum(flat[pl.ds(CP * i + params, n, stride=8 * CP), :], axis=0, keepdims=True) for i in range(3)]
        tally_out[k] = jnp.concatenate(sums + [jnp.zeros((5, G), f32)], axis=0)
        tally_sems = [new_sem(), new_sem()]
        rows8(tally_in.at[k], scene)[...] = tally_out[k]
        to_scene(lambda peer: tally_out.at[k], rows8(tally_in.at[k], scene), *tally_sems)

        def forward(t):
            v = jnp.concatenate(
                [z[k, ids[j, t]] for j in range(2)], axis=1)
            vh, vl = split2(v)
            lhs = jnp.concatenate([vh, vl, vh], axis=0)
            total = jnp.zeros((1, 2 * G), f32)
            for j in range(2):
                p = 2 * t + j
                projected = dot(lhs[:, G * j : G * (j + 1)], bst[t], TN)
                tint = jnp.transpose(v[:, G * j : G * (j + 1)])[:, params - 1 : params]
                total = total + jnp.sum(S[p] * projected + W[p] * tint, axis=0, keepdims=True)
            put_u(t, total)

        product = SceneSum(k + 1)
        product.run(forward, 4)
        wait(some8(tally_in.at[k]), tally_sems[1])
        wait(some8(tally_in.at[k]), tally_sems[0])
        tally = tally_in[k, pl.ds(0, 8), :]
        for i in range(1, n):
            tally = tally + tally_in[k, pl.ds(8 * i, 8), :]
        totals = lane_sum(tally)
        rz, zdz, zdp = totals[0:1], totals[1:2], totals[2:3]
        beta = rz / rz_old if k else 0.0 * one
        u = product.total()
        if k:
            u = u + beta * half_rows(u_now.at[k], mine)[...]
        if k + 1 < ITERS:
            product.publish(u)
        pdp = zdz + 2.0 * beta * zdp + beta * beta * pdp
        if k:
            direction[...] = z[k] + beta * direction[...]
            shard[Z] = zs + beta * shard[Z]
        else:
            direction[...] = z[k]
            shard[Z] = zs
        if k + 1 < ITERS:
            back = lambda t: apply_transpose(t, lanes(u_now.at[k + 1], 2 * t))
            half_loop(mine, back, 4)
            product.rest()
            half_loop(other, back, 4)
            scatter_blocks(k)
            square = jnp.sum(u_now[k + 1] * u_now[k + 1], axis=0, keepdims=True)
            w_out[k, :, params] = jnp.broadcast_to(square, (n, 8, G))
            image_sum = ViewScatter(k + 2, k)
            image_sum.start()
            image_sum.middle()
            w = image_sum.total()
            a = rz / (lane_sum(w[params, 0:1]) + pdp)
            image = w[:params] + (DAMPING * shard[D] + RIDGE) * shard[Z]
            shard[R] = shard[R] - a * image
        else:
            squares = rows8(dot_in, 2 * view + core)
            squares[...] = jnp.broadcast_to(jnp.sum(u * u, axis=0, keepdims=True), (8, G))
            dot_sems = [new_sem(), new_sem()]

            def share(d, c):
                there = lax.rem(view + d, n)
                push(squares, squares, *dot_sems, (there, scene))
                push(squares, squares, *dot_sems, (there, scene + 1 - 2 * core))
                return c

            push(squares, squares, *dot_sems, partner)
            lax.fori_loop(1, n, share, 0)
            wait(dot_in.at[pl.ds(0, 8 * (2 * n - 1))], dot_sems[1])
            wait(dot_in.at[pl.ds(0, 8 * (2 * n - 1))], dot_sems[0])
            total = dot_in[pl.ds(0, 8), :]
            for i in range(1, 2 * n):
                total = total + dot_in[pl.ds(8 * i, 8), :]
            a = rz / (lane_sum(total[0:1]) + pdp)
        if k + 1 == ITERS:
            for b in range(G):
                step[:, pl.ds(b * G, G)] = (total_step[b] + a * direction[b])[:params]
        elif k:
            total_step[...] = total_step[...] + a * direction[...]
        else:
            total_step[...] = a * direction[...]
        rz_old = rz


def local(n, params, pixel_basis, tile_blocks, depth_rank, target):
    count = params.shape[0]
    tiles, _, pixels = pixel_basis.shape
    ids = tile_blocks.transpose(1, 2, 0).reshape(2, tiles)
    basis = pixel_basis.transpose(1, 0, 2).reshape((count - 1) * tiles, pixels)
    vmem = pl.BlockSpec(memory_space=pltpu.VMEM)
    lists = 2 * tiles
    return pl.pallas_call(
        functools.partial(kernel, n, count, tiles),
        out_shape=(
            jax.ShapeDtypeStruct((count, G * G), f32),
            jax.ShapeDtypeStruct((tiles, pixels), f32),
        ),
        in_specs=[vmem, vmem, pl.BlockSpec(memory_space=pltpu.SMEM), vmem, vmem, vmem],
        out_specs=(vmem, vmem),
        scratch_shapes=[
            pltpu.VMEM((tiles, CP, pixels), f32),
            pltpu.VMEM((tiles, 3 * CP, pixels), bf16),
            pltpu.VMEM((lists, G, pixels), f32),
            pltpu.VMEM((lists, G, pixels), f32),
            pltpu.VMEM((lists, G, 2 * pixels), bf16),
            pltpu.VMEM((lists, G, 2 * pixels), bf16),
            pltpu.VMEM((CP * lists, G), f32),
            pltpu.VMEM((G, 2 * lists), bf16),
            pltpu.VMEM((8 * n, G), f32),
            pltpu.VMEM((8 * n, G), f32),
            pltpu.VMEM((8 * n, G), f32),
            pltpu.VMEM((8 * n, G), f32),
            pltpu.VMEM((2 * tiles, G), f32),
            pltpu.VMEM((ITERS + 1, tiles, G), f32),
            pltpu.VMEM((ITERS + 1, n // 2, tiles, G), f32),
            pltpu.VMEM((ITERS + 1, 2 * tiles, G), f32),
            pltpu.VMEM((ITERS, 8, G), f32),
            pltpu.VMEM((ITERS, 8 * n, G), f32),
            pltpu.VMEM((2, n, count + 1, 8, G), f32),
            pltpu.VMEM((ITERS + 1, SIDE - 1, SIDE, 8, 8, G), f32),
            pltpu.VMEM((ITERS + 1, SIDE - 1, SIDE, count - 7, 8, G), f32),
            pltpu.VMEM((ITERS + 1, SIDE, 8, 8, G), f32),
            pltpu.VMEM((ITERS + 1, SIDE, count - 7, 8, G), f32),
            pltpu.VMEM((ITERS + 1, SIDE - 1, 8, 8, G), f32),
            pltpu.VMEM((ITERS + 1, SIDE - 1, count - 7, 8, G), f32),
            pltpu.VMEM((ITERS, G, CP, G), f32),
            pltpu.VMEM((G, CP, G), f32),
            pltpu.VMEM((G, CP, G), f32),
            pltpu.VMEM((8 * CP, G), f32),
            pltpu.VMEM((ITERS, 8, CP, G), f32),
            pltpu.VMEM((4, count, 8, G), f32),
            pltpu.VMEM((16 * n, G), f32),
            pltpu.SemaphoreType.DMA((SEMS,)),
        ],
        compiler_params=pltpu.CompilerParams(
            collective_id=0, has_side_effects=True, vmem_limit_bytes=64 * 1024 * 1024 - 65536),
        name="lm_step",
    )(params, basis, ids, ids, depth_rank, target)


def solution(mesh):
    in_specs = (
        P(None, "scene"),
        P("view", None, None),
        P("view", "scene", None),
        P("view", None),
        P("view", None),
    )
    out_specs = (P(None, "scene"), P("view", None))
    step = functools.partial(local, mesh.shape["scene"])
    return jax.shard_map(step, mesh=mesh, in_specs=in_specs, out_specs=out_specs, check_vma=False)
```

```python
import functools

import jax
import jax.numpy as jnp
from jax import lax
from jax.experimental import pallas as pl
from jax.experimental.pallas import tpu as pltpu
from jax.sharding import PartitionSpec as P

MESH = pl.DeviceIdType.MESH
ALPHA = 0.004
DAMPING = 0.1
RIDGE = 0.0001
ITERS = 3
SIDE = 4
SEMS = 224
PARTS = ((0, 4, 8), (8, 11, 14))
G = 128
CP = 16
f32 = jnp.float32
bf16 = jnp.bfloat16
NT = (((1,), (1,)), ((), ()))
TN = (((0,), (0,)), ((), ()))


def split2(x):
    hi = x.astype(bf16)
    return hi, (x - hi.astype(f32)).astype(bf16)


def split3(x):
    hi = x.astype(bf16)
    rest = x - hi.astype(f32)
    mid = rest.astype(bf16)
    return hi, mid, (rest - mid.astype(f32)).astype(bf16)


def dot(a, b, dims=(((1,), (0,)), ((), ()))):
    return lax.dot_general(a, b, dims, preferred_element_type=f32)


def lanes(ref, row):
    return jnp.concatenate([ref[pl.ds(row, 1), :], ref[pl.ds(row + 1, 1), :]], axis=1)


def kernel(
    n, params, tiles,
    par, basis, ids, ids_rows, rank, target,
    base, last_direction, scale, residual,
    b16, bst, S, W, hi, lo, stk, onehot,
    bl_out, bl_in, fr_out, fr_in,
    u_out, u_pair, u_z, u_now, tally_out, tally_in,
    w_out, parts, half, last,
    z, z_in, direction, total_step, z_shard, shard, dot_in,
    sems,
):
    view = lax.axis_index("view")
    scene = lax.axis_index("scene")
    y, x = view // SIDE, lax.rem(view, SIDE)
    zz, core = scene // 2, lax.rem(scene, 2)
    partner = (view, scene + 1 - 2 * core)
    barrier = pltpu.get_barrier_semaphore()

    def greet(d, c):
        pl.semaphore_signal(barrier, inc=1, device_id=(lax.rem(view + d, n), scene), device_id_type=MESH)
        pl.semaphore_signal(barrier, inc=1, device_id=(lax.rem(view + d, n), scene + 1 - 2 * core), device_id_type=MESH)
        pl.semaphore_signal(barrier, inc=1, device_id=(view, lax.rem(scene + d, n)), device_id_type=MESH)
        return c

    lax.fori_loop(1, n, greet, 0)
    counter = iter(range(SEMS))
    new_sem = lambda: sems.at[next(counter)]

    def push(src, dst, send_sem, recv_sem, where):
        pltpu.make_async_remote_copy(
            src_ref=src, dst_ref=dst, send_sem=send_sem, recv_sem=recv_sem, device_id=where, device_id_type=MESH,
        ).start()

    def wait(ref, sem):
        pltpu.make_async_copy(ref, ref, sem).wait()

    def to_scene(src_of, dst, send_sem, recv_sem):
        def body(d, c):
            peer = lax.rem(scene + d, n)
            push(src_of(peer), dst, send_sem, recv_sem, (view, peer))
            return c

        lax.fori_loop(1, n, body, 0)

    block_at = lax.broadcasted_iota(jnp.int32, (G, tiles), 0)
    hot = [jnp.where(block_at == ids_rows[pl.ds(j, 1), :], 1.0, 0.0).astype(bf16) for j in range(2)]
    onehot[...] = jnp.concatenate(hot + hot, axis=1)
    below = lax.broadcasted_iota(jnp.int32, (G, G), 1) < lax.broadcasted_iota(jnp.int32, (G, G), 0)
    below = jnp.where(below, 1.0, 0.0).astype(bf16)
    below = jnp.concatenate([below, below], axis=1)

    halves = [w_out.at[h].reshape(n * params * 8, G) for h in range(2)]
    for h in range(2):
        halves[h][pl.ds(0, (params - 1) * tiles)] = basis[:, G * h : G * (h + 1)]

    def prepare(t, c):
        full = jnp.concatenate([half[pl.ds(t, params - 1, stride=tiles), :] for half in halves], axis=1)
        full = jnp.concatenate([full, jnp.zeros((CP - params + 1, full.shape[1]), f32)], axis=0)
        b16[t] = full
        bh, bl = split2(full)
        bst[t] = jnp.concatenate([bh, bh, bl], axis=0)
        return c

    lax.fori_loop(0, tiles, prepare, 0, unroll=4)

    def stage(b, c):
        piece = par[:, pl.ds(pl.multiple_of(b * G, G), G)]
        direction[b] = jnp.concatenate([piece, jnp.zeros((CP - params, G), f32)], axis=0)
        return c

    lax.fori_loop(0, G, stage, 0, unroll=8)
    z[:, params + 1 :] = jnp.zeros((G, CP - params - 1, G), f32)

    def listing_params(t, j):
        return direction[ids[j, t]]

    def slot_row(t, j):
        return 8 * (t // 2) + 4 * j + 2 * lax.rem(t, 2)

    def opacities(t, c):
        bh, bm, bl = split3(b16[t])
        rhs = jnp.concatenate([bh, bm, bh, bl, bh, bm], axis=0)
        for j in range(2):
            p = 2 * t + j
            vh, vm, vl = split3(listing_params(t, j))
            lhs = jnp.concatenate([vh, vh, vm, vh, vl, vm], axis=0)
            logit = dot(lhs, rhs, TN)
            o = ALPHA * (1.0 / (1.0 + jnp.exp(-logit)))
            keep = -o * (1.0 + o * (0.5 + o * (1.0 / 3.0 + o * 0.25)))
            W[p] = o
            kh, kl = split2(keep)
            hi[p] = kh
            lo[p] = kl
            total = jnp.sum(keep, axis=0, keepdims=True)
            r = slot_row(t, j)
            bl_out[pl.ds(r, 1), :] = total[:, :G]
            bl_out[pl.ds(r + 1, 1), :] = total[:, G:]
        return c

    lax.fori_loop(0, tiles, opacities, 0, unroll=4)

    pl.semaphore_wait(barrier, 3 * (n - 1))
    rows8 = lambda ref, i: ref.at[pl.ds(pl.multiple_of(i * 8, 8), 8)]
    some8 = lambda ref: ref.at[pl.ds(0, 8 * (n - 1))]
    front_sems = [new_sem() for _ in range(4)]
    to_scene(lambda peer: rows8(bl_out, peer), rows8(bl_in, scene), front_sems[0], front_sems[1])
    rows8(bl_in, scene)[...] = rows8(bl_out, scene)[...]

    def weights(t, c):
        for j in range(2):
            p = 2 * t + j
            keeps = jnp.concatenate([hi[p], lo[p]], axis=0)
            inner = dot(below, keeps)
            o = W[p]
            colour = jnp.transpose(listing_params(t, j))[:, params - 1 : params]
            w = jnp.exp(inner) * o
            W[p] = w
            S[p] = w * colour * (1.0 - o * (1.0 / ALPHA))
        return c

    lax.fori_loop(0, tiles // 2, weights, 0, unroll=4)

    wait(some8(bl_in), front_sems[1])
    wait(some8(bl_out), front_sems[0])
    slots = 2 * n
    eye = lax.broadcasted_iota(jnp.int32, (slots, slots), 0) == lax.broadcasted_iota(jnp.int32, (slots, slots), 1)
    for i in range(2):
        rank_row = jnp.broadcast_to(rank[pl.ds(2 * scene + i, 1), :].astype(f32), (slots, slots))
        rank_col = jnp.sum(jnp.where(eye, rank_row, 0.0), axis=1, keepdims=True)
        earlier = jnp.where(rank_row < rank_col, 1.0, 0.0).astype(bf16)
        for h in range(2):
            lh, lm, ll = split3(bl_in[pl.ds(2 * i + h, slots, stride=4), :])
            front = dot(earlier, lh) + dot(earlier, lm) + dot(earlier, ll)
            fr_out[pl.ds(2 * i + h, slots, stride=4), :] = jnp.exp(front)
    to_scene(lambda peer: rows8(fr_out, peer), rows8(fr_in, scene), front_sems[2], front_sems[3])
    rows8(fr_in, scene)[...] = rows8(fr_out, scene)[...]

    lax.fori_loop(tiles // 2, tiles, weights, 0, unroll=4)
    wait(some8(fr_in), front_sems[3])
    wait(some8(fr_out), front_sems[2])

    def put_u(t, value):
        u_out[pl.ds(2 * t, 1), :] = value[:, :G]
        u_out[pl.ds(2 * t + 1, 1), :] = value[:, G:]

    mine, other = core * (tiles // 2), (1 - core) * (tiles // 2)

    def half_loop(first, body, unroll):
        def step_of(i, c):
            body(first + i)
            return c

        lax.fori_loop(0, tiles // 2, step_of, 0, unroll=unroll)

    def finish(t):
        total = jnp.zeros((1, 2 * G), f32)
        for j in range(2):
            p = 2 * t + j
            factor = lanes(fr_in, slot_row(t, j))
            w = W[p] * factor
            s = S[p] * factor
            W[p] = w
            S[p] = s
            hi[p], lo[p] = split2(s)
            colour = jnp.transpose(listing_params(t, j))[:, params - 1 : params]
            total = total + jnp.sum(w * colour, axis=0, keepdims=True)
        put_u(t, total)

    def rows_of(part, more=0):
        a, b, end = PARTS[part]
        end = end + more * part
        return pl.ds(a, b - a), pl.ds(b, end - b), pl.ds(a, end - a)

    at_x = lambda d: (y * SIDE + lax.rem(x + d, SIDE), scene)
    at_y = lambda d: (lax.rem(y + d, SIDE) * SIDE + x, scene)

    half_rows = lambda ref, first: ref.at[pl.ds(pl.multiple_of(2 * first, 8), tiles)]

    class SceneSum:
        def __init__(self, q):
            self.q, self.sems = q, [new_sem() for _ in range(6)]

        def run(self, body, unroll):
            q, sem = self.q, self.sems
            half_loop(other, body, unroll)
            push(half_rows(u_out, other), u_pair.at[q], sem[0], sem[1], partner)
            half_loop(mine, body, unroll)
            wait(u_pair.at[q], sem[1])
            u_z[q, zz] = half_rows(u_out, mine)[...] + u_pair[q]
            for d in (4, 3, 5, 2, 6, 1, 7):
                push(u_z.at[q, zz], u_z.at[q, zz], sem[2], sem[3], (view, lax.rem(scene + 2 * d, n)))
            wait(u_pair.at[q], sem[0])

        def total(self):
            q, sem = self.q, self.sems
            wait(u_z.at[q, pl.ds(0, n // 2 - 1)], sem[3])
            wait(u_z.at[q, pl.ds(0, n // 2 - 1)], sem[2])
            out = u_z[q, 0]
            for i in range(1, n // 2):
                out = out + u_z[q, i]
            return out

        def publish(self, value):
            q, sem = self.q, self.sems
            rows = half_rows(u_now.at[q], mine)
            rows[...] = value
            push(rows, rows, sem[4], sem[5], partner)

        def rest(self):
            q, sem = self.q, self.sems
            wait(half_rows(u_now.at[q], other), sem[5])
            wait(half_rows(u_now.at[q], other), sem[4])

    render = SceneSum(0)
    render.run(finish, 2)

    def scatter_blocks(slot):
        for c in range(0, params, 2):
            x = jnp.concatenate([stk[pl.ds((c + e) * 2 * tiles, 2 * tiles), :] for e in range(2)], axis=1)
            xh, xl = split2(x)
            out = dot(onehot[...], jnp.concatenate([xh, xl], axis=0))
            w_out[slot, :, c] = out[:, :G].reshape(n, 8, G)
            w_out[slot, :, c + 1] = out[:, G:].reshape(n, 8, G)

    def put_listing(t, value):
        for j in range(2):
            stk[pl.ds(tiles * j + t, CP, stride=2 * tiles), :] = value[:, G * j : G * (j + 1)]

    class ViewScatter:
        def __init__(self, q, slot):
            self.q, self.slot = q, slot
            self.send_sem = [new_sem() for _ in PARTS]
            self.last = [[new_sem(), new_sem()] for _ in PARTS]
            self.first = [[[new_sem() for _ in range(SIDE)] for _ in range(2)] for _ in PARTS]

        def start(self, part):
            q, slot = self.q, self.slot
            row_a, row_b, _ = rows_of(part)
            for e in (2, 1, 3, 0):
                for d in (2, 1, 3):
                    to_x, to_y = lax.rem(x + d, SIDE), lax.rem(y + d, SIDE)
                    line_y, line_x = lax.rem(y + e, SIDE), lax.rem(x + e, SIDE)
                    push(w_out.at[slot, line_y * SIDE + to_x, row_a], parts.at[q, d - 1, line_y, row_a],
                         self.send_sem[part], self.first[part][0][e], (y * SIDE + to_x, scene))
                    push(w_out.at[slot, to_y * SIDE + line_x, row_b], parts.at[q, d - 1, line_x, row_b],
                         self.send_sem[part], self.first[part][1][e], (to_y * SIDE + x, scene))

        def middle(self, part):
            q, slot = self.q, self.slot
            row_a, row_b, _ = rows_of(part)
            for e in (2, 1, 3, 0):
                line_y, line_x = lax.rem(y + e, SIDE), lax.rem(x + e, SIDE)
                for own, line, row, way, to in (
                    (line_y * SIDE + x, line_y, row_a, 0, line_y * SIDE + x),
                    (y * SIDE + line_x, line_x, row_b, 1, y * SIDE + line_x),
                ):
                    wait(parts.at[q, :, line, row], self.first[part][way][e])
                    total = w_out[slot, own, row] + parts[q, 0, line, row]
                    half[q, line, row] = total + parts[q, 1, line, row] + parts[q, 2, line, row]
                    if e:
                        push(half.at[q, line, row], last.at[q, e - 1, row],
                             self.send_sem[part], self.last[part][way], (to, scene))

        def total(self, part):
            q, slot = self.q, self.slot
            row_a, row_b, row = rows_of(part)
            wait(last.at[q, :, row_a], self.last[part][0])
            wait(last.at[q, :, row_b], self.last[part][1])
            wait(w_out.at[slot, pl.ds(0, n - 1), row], self.send_sem[part])
            out_a, out_b = half[q, y, row_a], half[q, x, row_b]
            for d in range(SIDE - 1):
                out_a, out_b = out_a + last[q, d, row_a], out_b + last[q, d, row_b]
            return jnp.concatenate([out_a, out_b], axis=0)

    class ViewGather:
        def __init__(self, k):
            self.k = k
            self.send_sem, self.rest = [new_sem() for _ in PARTS], [new_sem() for _ in PARTS]
            self.near = [[[new_sem() for _ in range(SIDE - 1)] for _ in range(2)] for _ in PARTS]

        def start(self, part):
            k = self.k
            row_a, row_b, row = rows_of(part, 1)
            z_in[k, view, row] = z_shard[k, row]
            src_a, src_b = z_shard.at[k, row_a], z_shard.at[k, row_b]
            dst_a, dst_b = z_in.at[k, view, row_a], z_in.at[k, view, row_b]
            send_sem, rest = self.send_sem[part], self.rest[part]
            for d in (1, 3, 2):
                push(src_a, dst_a, send_sem, self.near[part][0][d - 1], at_x(d))
                push(src_b, dst_b, send_sem, self.near[part][1][d - 1], at_y(d))
            for d in (1, 3, 2):
                push(src_b, dst_b, send_sem, rest, at_x(d))
                push(src_a, dst_a, send_sem, rest, at_y(d))

        def relay(self, part):
            k = self.k
            row_a, row_b, _ = rows_of(part, 1)
            send_sem, rest = self.send_sem[part], self.rest[part]
            for d in (1, 3, 2):
                from_x = y * SIDE + lax.rem(x + SIDE - d, SIDE)
                from_y = lax.rem(y + SIDE - d, SIDE) * SIDE + x
                there_a, there_b = z_in.at[k, from_x, row_a], z_in.at[k, from_y, row_b]
                wait(there_a, self.near[part][0][d - 1])
                for e in (2, 1, 3):
                    push(there_a, there_a, send_sem, rest, at_y(e))
                wait(there_b, self.near[part][1][d - 1])
                for e in (2, 1, 3):
                    push(there_b, there_b, send_sem, rest, at_x(e))

        def finish(self, part):
            k = self.k
            row = rows_of(part, 1)[2]
            wait(z_in.at[k, pl.ds(0, 12), row], self.rest[part])
            wait(z_in.at[k, pl.ds(0, 15), row], self.send_sem[part])
            flat = z_in.at[k].reshape(n * (params + 1) * 8, G)
            first, count = row.start, row.size

            def restage(owner, c):
                for i in range(8):
                    at = owner * (params + 1) * 8 + first * 8 + i
                    z[8 * owner + i, pl.ds(first, count)] = flat[pl.ds(at, count, stride=8), :]
                return c

            lax.fori_loop(0, n, restage, 0, unroll=4)

    colour_row = lax.broadcasted_iota(jnp.int32, (CP, 2 * G), 0) == params - 1
    colour_row = jnp.where(colour_row, 1.0, 0.0).astype(bf16)

    def transpose_rows(left, right_hi, right_lo, tinted):
        lh, ll = split2(left)
        first = dot(jnp.concatenate([lh, ll], axis=0), right_hi, NT)
        tinted = tinted[:, :G] + tinted[:, G:]
        last = dot(colour_row, jnp.concatenate(split2(tinted), axis=1), NT)
        return first[:CP] + first[CP:] + dot(lh, right_lo, NT) + last

    def pair(ref, t):
        return jnp.concatenate([ref[2 * t], ref[2 * t + 1]], axis=0)

    def diagonal(t, c):
        s, w = pair(S, t), pair(W, t)
        put_listing(t, transpose_rows(b16[t] * b16[t], *split2(s * s), w * w))
        return c

    lax.fori_loop(0, tiles, diagonal, 0, unroll=4)
    scatter_blocks(0)
    diag_sum = ViewScatter(0, 0)
    for part in range(2):
        diag_sum.start(part)
    render.publish(render.total())

    def apply_transpose(t, u):
        put_listing(t, transpose_rows(b16[t] * u, pair(hi, t), pair(lo, t), pair(W, t) * u))

    def gradient(t):
        u = lanes(u_now.at[0], 2 * t) - target[pl.ds(t, 1), :]
        residual[pl.ds(t, 1), :] = u
        apply_transpose(t, u)

    half_loop(mine, gradient, 8)
    for part in range(2):
        diag_sum.middle(part)
    render.rest()
    half_loop(other, gradient, 8)
    scatter_blocks(1)
    grad_sum = ViewScatter(1, 1)
    for part in range(2):
        grad_sum.start(part)

    R, P_, D = 0, 1, 2

    def lane_sum(x):
        return jnp.sum(x, axis=1, keepdims=True)

    def fold(x):
        return jnp.sum(jnp.sum(x, axis=0), axis=0, keepdims=True)

    for part in range(2):
        shard[D, rows_of(part)[2]] = diag_sum.total(part)
    for part in range(2):
        grad_sum.middle(part)

    def next_z(k, remainder):
        gather = ViewGather(k)
        inner = [jnp.zeros((1, G), f32)] * 3
        for part in range(2):
            row = rows_of(part)[2]
            r = remainder(part, row)
            shard[R, row] = r
            d = shard[D, row]
            zs = r / ((1.0 + DAMPING) * d + RIDGE)
            dz = (DAMPING * d + RIDGE) * zs
            inner = [inner[0] + fold(r * zs), inner[1] + fold(zs * dz), inner[2] + fold(shard[P_, row] * dz) if k else inner[2]]
            z_shard[k, row] = zs
            if part:
                z_shard[k, params] = jnp.concatenate(inner + [jnp.zeros((5, G), f32)], axis=0)
            gather.start(part)
        gather.relay(0)
        gather.relay(1)
        gather.finish(0)
        gather.finish(1)

    def share_square(k, u):
        squares = rows8(dot_in.at[k], 2 * view + core)
        squares[...] = jnp.broadcast_to(jnp.sum(u * u, axis=0, keepdims=True), (8, G))
        pair_sems = [new_sem(), new_sem()]

        def share(d, c):
            there = lax.rem(view + d, n)
            push(squares, squares, *pair_sems, (there, scene))
            push(squares, squares, *pair_sems, (there, scene + 1 - 2 * core))
            return c

        push(squares, squares, *pair_sems, partner)
        lax.fori_loop(1, n, share, 0)
        return pair_sems

    def all_squares(k, pair_sems):
        wait(dot_in.at[k, pl.ds(0, 8 * (2 * n - 1))], pair_sems[1])
        wait(dot_in.at[k, pl.ds(0, 8 * (2 * n - 1))], pair_sems[0])
        total = dot_in[k, pl.ds(0, 8), :]
        for i in range(1, 2 * n):
            total = total + dot_in[k, pl.ds(8 * i, 8), :]
        return lane_sum(total[0:1])

    one = jnp.ones((1, 1), f32)
    rz_old, pdp = one, 0.0 * one
    remainder = lambda part, row: -grad_sum.total(part)
    for k in range(ITERS):
        next_z(k, remainder)
        tally = z_in[k, 0, params]
        for i in range(1, n):
            tally = tally + z_in[k, i, params]
        tally_out[k] = tally
        tally_sems = [new_sem(), new_sem()]
        rows8(tally_in.at[k], scene)[...] = tally_out[k]
        to_scene(lambda peer: tally_out.at[k], rows8(tally_in.at[k], scene), *tally_sems)

        def forward(t):
            v = jnp.concatenate(
                [z[ids[j, t]] for j in range(2)], axis=1)
            vh, vl = split2(v)
            lhs = jnp.concatenate([vh, vl, vh], axis=0)
            total = jnp.zeros((1, 2 * G), f32)
            for j in range(2):
                p = 2 * t + j
                projected = dot(lhs[:, G * j : G * (j + 1)], bst[t], TN)
                tint = jnp.transpose(v[:, G * j : G * (j + 1)])[:, params - 1 : params]
                total = total + jnp.sum(S[p] * projected + W[p] * tint, axis=0, keepdims=True)
            put_u(t, total)

        product = SceneSum(k + 1)
        product.run(forward, 8)
        wait(some8(tally_in.at[k]), tally_sems[1])
        wait(some8(tally_in.at[k]), tally_sems[0])
        tally = tally_in[k, pl.ds(0, 8), :]
        for i in range(1, n):
            tally = tally + tally_in[k, pl.ds(8 * i, 8), :]
        totals = lane_sum(tally)
        rz, zdz, zdp = totals[0:1], totals[1:2], totals[2:3]
        beta = rz / rz_old if k else 0.0 * one
        u = product.total()
        if k:
            u = u + beta * half_rows(u_now.at[k], mine)[...]
        if k + 1 < ITERS:
            product.publish(u)
        pdp = zdz + 2.0 * beta * zdp + beta * beta * pdp
        pair_sems = share_square(k, u)
        if k:
            direction[...] = z[...] + beta * direction[...]
            shard[P_] = z_shard[k, pl.ds(0, params)] + beta * shard[P_]
        else:
            direction[...] = z[...]
            shard[P_] = z_shard[k, pl.ds(0, params)]
        if k + 1 < ITERS:
            back = lambda t: apply_transpose(t, lanes(u_now.at[k + 1], 2 * t))
            half_loop(mine, back, 8)
            product.rest()
            half_loop(other, back, 8)
            scatter_blocks(k)
            image_sum = ViewScatter(k + 2, k)
            image_sum.start(0)
            image_sum.start(1)
            a = rz / (all_squares(k, pair_sems) + pdp)
            image_sum.middle(0)
            image_sum.middle(1)

            def remainder(part, row, image_sum=image_sum, a=a):
                image = image_sum.total(part) + (DAMPING * shard[D, row] + RIDGE) * shard[P_, row]
                return shard[R, row] - a * image

            if k:
                total_step[...] = total_step[...] + a * direction[...]
            else:
                total_step[...] = a * direction[...]
        else:
            def put_step(b, c):
                at = pl.ds(pl.multiple_of(b * G, G), G)
                base[:, at] = total_step[b][:params]
                last_direction[:, at] = direction[b][:params]
                return c

            lax.fori_loop(0, G, put_step, 0, unroll=8)
            a = rz / (all_squares(k, pair_sems) + pdp)
            scale[...] = jnp.broadcast_to(a, scale.shape)
        rz_old = rz


def local(n, params, pixel_basis, tile_blocks, depth_rank, target):
    count = params.shape[0]
    tiles, _, pixels = pixel_basis.shape
    ids = tile_blocks.transpose(1, 2, 0).reshape(2, tiles)
    basis = pixel_basis.transpose(1, 0, 2).reshape((count - 1) * tiles, pixels)
    vmem = pl.BlockSpec(memory_space=pltpu.VMEM)
    lists = 2 * tiles
    base, direction, scale, residual = pl.pallas_call(
        functools.partial(kernel, n, count, tiles),
        out_shape=(
            jax.ShapeDtypeStruct((count, G * G), f32),
            jax.ShapeDtypeStruct((count, G * G), f32),
            jax.ShapeDtypeStruct((1, G * G), f32),
            jax.ShapeDtypeStruct((tiles, pixels), f32),
        ),
        in_specs=[vmem, vmem, pl.BlockSpec(memory_space=pltpu.SMEM), vmem, vmem, vmem],
        out_specs=(vmem,) * 4,
        scratch_shapes=[
            pltpu.VMEM((tiles, CP, pixels), f32),
            pltpu.VMEM((tiles, 3 * CP, pixels), bf16),
            pltpu.VMEM((lists, G, pixels), f32),
            pltpu.VMEM((lists, G, pixels), f32),
            pltpu.VMEM((lists, G, pixels), bf16),
            pltpu.VMEM((lists, G, pixels), bf16),
            pltpu.VMEM((CP * lists, G), f32),
            pltpu.VMEM((G, 2 * lists), bf16),
            pltpu.VMEM((8 * n, G), f32),
            pltpu.VMEM((8 * n, G), f32),
            pltpu.VMEM((8 * n, G), f32),
            pltpu.VMEM((8 * n, G), f32),
            pltpu.VMEM((2 * tiles, G), f32),
            pltpu.VMEM((ITERS + 1, tiles, G), f32),
            pltpu.VMEM((ITERS + 1, n // 2, tiles, G), f32),
            pltpu.VMEM((ITERS + 1, 2 * tiles, G), f32),
            pltpu.VMEM((ITERS, 8, G), f32),
            pltpu.VMEM((ITERS, 8 * n, G), f32),
            pltpu.VMEM((2, n, count, 8, G), f32),
            pltpu.VMEM((ITERS + 1, SIDE - 1, SIDE, count, 8, G), f32),
            pltpu.VMEM((ITERS + 1, SIDE, count, 8, G), f32),
            pltpu.VMEM((ITERS + 1, SIDE - 1, count, 8, G), f32),
            pltpu.VMEM((G, CP, G), f32),
            pltpu.VMEM((ITERS, n, count + 1, 8, G), f32),
            pltpu.VMEM((G, CP, G), f32),
            pltpu.VMEM((G, CP, G), f32),
            pltpu.VMEM((ITERS, count + 1, 8, G), f32),
            pltpu.VMEM((3, count, 8, G), f32),
            pltpu.VMEM((ITERS, 16 * n, G), f32),
            pltpu.SemaphoreType.DMA((SEMS,)),
        ],
        compiler_params=pltpu.CompilerParams(
            collective_id=0, has_side_effects=True, vmem_limit_bytes=64 * 1024 * 1024 - 65536),
        name="lm_step",
    )(params, basis, ids, ids, depth_rank, target)
    return base + scale * direction, residual


def solution(mesh):
    in_specs = (
        P(None, "scene"),
        P("view", None, None),
        P("view", "scene", None),
        P("view", None),
        P("view", None),
    )
    out_specs = (P(None, "scene"), P("view", None))
    step = functools.partial(local, mesh.shape["scene"])
    return jax.shard_map(step, mesh=mesh, in_specs=in_specs, out_specs=out_specs, check_vma=False)
```

```python
import functools

import jax
import jax.numpy as jnp
from jax import lax
from jax.experimental import pallas as pl
from jax.experimental.pallas import tpu as pltpu
from jax.sharding import PartitionSpec as P

MESH = pl.DeviceIdType.MESH
ALPHA = 0.004
DAMPING = 0.1
RIDGE = 0.0001
ITERS = 3
SIDE = 4
SEMS = 224
PARTS = ((0, 4, 8), (8, 11, 14))
G = 128
CP = 16
f32 = jnp.float32
bf16 = jnp.bfloat16
NT = (((1,), (1,)), ((), ()))
TN = (((0,), (0,)), ((), ()))


def split2(x):
    hi = x.astype(bf16)
    return hi, (x - hi.astype(f32)).astype(bf16)


def split3(x):
    hi = x.astype(bf16)
    rest = x - hi.astype(f32)
    mid = rest.astype(bf16)
    return hi, mid, (rest - mid.astype(f32)).astype(bf16)


def dot(a, b, dims=(((1,), (0,)), ((), ()))):
    return lax.dot_general(a, b, dims, preferred_element_type=f32)


def lanes(ref, row):
    return jnp.concatenate([ref[pl.ds(row, 1), :], ref[pl.ds(row + 1, 1), :]], axis=1)


def kernel(
    n, params, tiles,
    par, basis, ids, ids_rows, rank, target,
    base, last_direction, scale, residual,
    b16, bst, S, W, hi, lo, stk, onehot,
    bl_out, bl_in, fr_out, fr_in,
    u_out, u_pair, u_z, u_now, tally_out, tally_in,
    w_out, parts, half, last,
    z, z_in, direction, total_step, z_shard, shard, dot_in,
    sems,
):
    view = lax.axis_index("view")
    scene = lax.axis_index("scene")
    y, x = view // SIDE, lax.rem(view, SIDE)
    zz, core = scene // 2, lax.rem(scene, 2)
    partner = (view, scene + 1 - 2 * core)
    xs = [lax.rem(x + d, SIDE) for d in range(SIDE)]
    ys = [lax.rem(y + d, SIDE) for d in range(SIDE)]
    barrier = pltpu.get_barrier_semaphore()

    def greet(d, c):
        pl.semaphore_signal(barrier, inc=1, device_id=(lax.rem(view + d, n), scene), device_id_type=MESH)
        pl.semaphore_signal(barrier, inc=1, device_id=(lax.rem(view + d, n), scene + 1 - 2 * core), device_id_type=MESH)
        pl.semaphore_signal(barrier, inc=1, device_id=(view, lax.rem(scene + d, n)), device_id_type=MESH)
        return c

    lax.fori_loop(1, n, greet, 0)
    counter = iter(range(SEMS))
    new_sem = lambda: sems.at[next(counter)]

    def push(src, dst, send_sem, recv_sem, where):
        pltpu.make_async_remote_copy(
            src_ref=src, dst_ref=dst, send_sem=send_sem, recv_sem=recv_sem, device_id=where, device_id_type=MESH,
        ).start()

    def wait(ref, sem):
        pltpu.make_async_copy(ref, ref, sem).wait()

    def to_scene(src_of, dst, send_sem, recv_sem):
        def body(d, c):
            peer = lax.rem(scene + d, n)
            push(src_of(peer), dst, send_sem, recv_sem, (view, peer))
            return c

        lax.fori_loop(1, n, body, 0)

    below = lax.broadcasted_iota(jnp.int32, (G, G), 1) < lax.broadcasted_iota(jnp.int32, (G, G), 0)
    below = jnp.where(below, 1.0, 0.0).astype(bf16)
    below = jnp.concatenate([below, below], axis=1)

    halves = [w_out.at[h].reshape(n * params * 8, G) for h in range(2)]
    for h in range(2):
        halves[h][pl.ds(0, (params - 1) * tiles)] = basis[:, G * h : G * (h + 1)]

    def prepare(t, c):
        full = jnp.concatenate([half[pl.ds(t, params - 1, stride=tiles), :] for half in halves], axis=1)
        full = jnp.concatenate([full, jnp.zeros((CP - params + 1, full.shape[1]), f32)], axis=0)
        b16[t] = full
        return c

    lax.fori_loop(0, tiles, prepare, 0, unroll=4)

    def stage(b, c):
        piece = par[:, pl.ds(pl.multiple_of(b * G, G), G)]
        direction[b] = jnp.concatenate([piece, jnp.zeros((CP - params, G), f32)], axis=0)
        return c

    lax.fori_loop(0, G, stage, 0, unroll=8)
    z[:, params + 1 :] = jnp.zeros((G, CP - params - 1, G), f32)

    def listing_params(t, j):
        return direction[ids[j, t]]

    def slot_row(t, j):
        return 8 * (t // 2) + 4 * j + 2 * lax.rem(t, 2)

    def opacities(t, c):
        bh, bm, bl = split3(b16[t])
        rhs = jnp.concatenate([bh, bm, bh, bl, bh, bm], axis=0)
        for j in range(2):
            p = 2 * t + j
            vh, vm, vl = split3(listing_params(t, j))
            lhs = jnp.concatenate([vh, vh, vm, vh, vl, vm], axis=0)
            logit = dot(lhs, rhs, TN)
            o = ALPHA * (1.0 / (1.0 + jnp.exp(-logit)))
            keep = -o * (1.0 + o * (0.5 + o * (1.0 / 3.0 + o * 0.25)))
            W[p] = o
            kh, kl = split2(keep)
            hi[p] = kh
            lo[p] = kl
            total = jnp.sum(keep, axis=0, keepdims=True)
            r = slot_row(t, j)
            bl_out[pl.ds(r, 1), :] = total[:, :G]
            bl_out[pl.ds(r + 1, 1), :] = total[:, G:]
        return c

    lax.fori_loop(0, tiles, opacities, 0, unroll=4)

    pl.semaphore_wait(barrier, 3 * (n - 1))
    rows8 = lambda ref, i: ref.at[pl.ds(pl.multiple_of(i * 8, 8), 8)]
    some8 = lambda ref: ref.at[pl.ds(0, 8 * (n - 1))]
    front_sems = [new_sem() for _ in range(4)]
    to_scene(lambda peer: rows8(bl_out, peer), rows8(bl_in, scene), front_sems[0], front_sems[1])
    rows8(bl_in, scene)[...] = rows8(bl_out, scene)[...]

    block_at = lax.broadcasted_iota(jnp.int32, (G, tiles), 0)
    hot = [jnp.where(block_at == ids_rows[pl.ds(j, 1), :], 1.0, 0.0).astype(bf16) for j in range(2)]
    onehot[...] = jnp.concatenate(hot + hot, axis=1)

    def basis_halves(t, c):
        bh, bl = split2(b16[t])
        bst[t] = jnp.concatenate([bh, bh, bl], axis=0)
        return c

    lax.fori_loop(0, tiles, basis_halves, 0, unroll=4)

    def weights(t, c):
        for j in range(2):
            p = 2 * t + j
            keeps = jnp.concatenate([hi[p], lo[p]], axis=0)
            inner = dot(below, keeps)
            o = W[p]
            colour = jnp.transpose(listing_params(t, j))[:, params - 1 : params]
            w = jnp.exp(inner) * o
            W[p] = w
            S[p] = w * colour * (1.0 - o * (1.0 / ALPHA))
        return c

    lax.fori_loop(0, tiles // 4, weights, 0, unroll=4)

    wait(some8(bl_in), front_sems[1])
    wait(some8(bl_out), front_sems[0])
    slots = 2 * n
    eye = lax.broadcasted_iota(jnp.int32, (slots, slots), 0) == lax.broadcasted_iota(jnp.int32, (slots, slots), 1)
    for i in range(2):
        rank_row = jnp.broadcast_to(rank[pl.ds(2 * scene + i, 1), :].astype(f32), (slots, slots))
        rank_col = jnp.sum(jnp.where(eye, rank_row, 0.0), axis=1, keepdims=True)
        earlier = jnp.where(rank_row < rank_col, 1.0, 0.0).astype(bf16)
        for h in range(2):
            lh, lm, ll = split3(bl_in[pl.ds(2 * i + h, slots, stride=4), :])
            front = dot(earlier, lh) + dot(earlier, lm) + dot(earlier, ll)
            fr_out[pl.ds(2 * i + h, slots, stride=4), :] = jnp.exp(front)
    to_scene(lambda peer: rows8(fr_out, peer), rows8(fr_in, scene), front_sems[2], front_sems[3])
    rows8(fr_in, scene)[...] = rows8(fr_out, scene)[...]

    lax.fori_loop(tiles // 4, tiles, weights, 0, unroll=4)
    wait(some8(fr_in), front_sems[3])
    wait(some8(fr_out), front_sems[2])

    def put_u(t, value):
        u_out[pl.ds(2 * t, 1), :] = value[:, :G]
        u_out[pl.ds(2 * t + 1, 1), :] = value[:, G:]

    mine, other = core * (tiles // 2), (1 - core) * (tiles // 2)

    def half_loop(first, body, unroll):
        def step_of(i, c):
            body(first + i)
            return c

        lax.fori_loop(0, tiles // 2, step_of, 0, unroll=unroll)

    def finish(t):
        total = jnp.zeros((1, 2 * G), f32)
        for j in range(2):
            p = 2 * t + j
            factor = lanes(fr_in, slot_row(t, j))
            w = W[p] * factor
            s = S[p] * factor
            W[p] = w
            S[p] = s
            hi[p], lo[p] = split2(s)
            colour = jnp.transpose(listing_params(t, j))[:, params - 1 : params]
            total = total + jnp.sum(w * colour, axis=0, keepdims=True)
        put_u(t, total)

    def rows_of(part, more=0):
        a, b, end = PARTS[part]
        end = end + more * part
        return pl.ds(a, b - a), pl.ds(b, end - b), pl.ds(a, end - a)

    row_to = [y * SIDE + xs[d] for d in range(SIDE)]
    column_to = [ys[d] * SIDE + x for d in range(SIDE)]
    at_x = lambda d: (row_to[d], scene)
    at_y = lambda d: (column_to[d], scene)

    half_rows = lambda ref, first: ref.at[pl.ds(pl.multiple_of(2 * first, 8), tiles)]

    class SceneSum:
        def __init__(self, q):
            self.q, self.sems = q, [new_sem() for _ in range(7)]

        def run(self, body, unroll):
            q, sem = self.q, self.sems
            quarter = tiles // 4

            def part_loop(first):
                def step_of(i, c):
                    body(first + i)
                    return c

                lax.fori_loop(0, quarter, step_of, 0, unroll=unroll)

            rows = lambda ref, first: ref.at[pl.ds(pl.multiple_of(2 * first, 8), 2 * quarter)]
            for i in range(2):
                part_loop(other + i * quarter)
                push(rows(u_out, other + i * quarter), rows(u_pair.at[q], i * quarter), sem[0], sem[1 + 5 * i], partner)
            for i in range(2):
                part_loop(mine + i * quarter)
                pair_rows, z_rows = rows(u_pair.at[q], i * quarter), rows(u_z.at[q, zz], i * quarter)
                wait(pair_rows, sem[1 + 5 * i])
                z_rows[...] = rows(u_out, mine + i * quarter)[...] + pair_rows[...]
                for d in (4, 3, 5, 2, 6, 1, 7):
                    push(z_rows, z_rows, sem[2], sem[3], (view, lax.rem(scene + 2 * d, n)))
            wait(u_pair.at[q], sem[0])

        def total(self):
            q, sem = self.q, self.sems
            wait(u_z.at[q, pl.ds(0, n // 2 - 1)], sem[3])
            wait(u_z.at[q, pl.ds(0, n // 2 - 1)], sem[2])
            out = u_z[q, 0]
            for i in range(1, n // 2):
                out = out + u_z[q, i]
            return out

        def publish(self, value):
            q, sem = self.q, self.sems
            rows = half_rows(u_now.at[q], mine)
            rows[...] = value
            push(rows, rows, sem[4], sem[5], partner)

        def rest(self):
            q, sem = self.q, self.sems
            wait(half_rows(u_now.at[q], other), sem[5])
            wait(half_rows(u_now.at[q], other), sem[4])

    render = SceneSum(0)
    render.run(finish, 2)

    def scatter_blocks(slot):
        for c in range(0, params, 2):
            x = jnp.concatenate([stk[pl.ds((c + e) * 2 * tiles, 2 * tiles), :] for e in range(2)], axis=1)
            xh, xl = split2(x)
            out = dot(onehot[...], jnp.concatenate([xh, xl], axis=0))
            w_out[slot, :, c] = out[:, :G].reshape(n, 8, G)
            w_out[slot, :, c + 1] = out[:, G:].reshape(n, 8, G)

    def put_listing(t, value):
        for j in range(2):
            stk[pl.ds(tiles * j + t, CP, stride=2 * tiles), :] = value[:, G * j : G * (j + 1)]

    class ViewScatter:
        def __init__(self, q, slot):
            self.q, self.slot = q, slot
            self.send_sem = [new_sem() for _ in PARTS]
            self.last = [[new_sem(), new_sem()] for _ in PARTS]
            self.first = [[[new_sem() for _ in range(SIDE)] for _ in range(2)] for _ in PARTS]

        def start(self, part):
            q, slot = self.q, self.slot
            row_a, row_b, _ = rows_of(part)
            for e in (2, 1, 3, 0):
                for d in (2, 1, 3):
                    to_x, to_y, line_y, line_x = xs[d], ys[d], ys[e], xs[e]
                    push(w_out.at[slot, line_y * SIDE + to_x, row_a], parts.at[q, d - 1, line_y, row_a],
                         self.send_sem[part], self.first[part][0][e], at_x(d))
                    push(w_out.at[slot, to_y * SIDE + line_x, row_b], parts.at[q, d - 1, line_x, row_b],
                         self.send_sem[part], self.first[part][1][e], at_y(d))

        def middle(self, part):
            q, slot = self.q, self.slot
            row_a, row_b, _ = rows_of(part)
            for e in (2, 1, 3, 0):
                for own, line, row, way in ((column_to[e], ys[e], row_a, 0), (row_to[e], xs[e], row_b, 1)):
                    wait(parts.at[q, :, line, row], self.first[part][way][e])
                    total = w_out[slot, own, row] + parts[q, 0, line, row]
                    half[q, line, row] = total + parts[q, 1, line, row] + parts[q, 2, line, row]
                    if e:
                        push(half.at[q, line, row], last.at[q, e - 1, row],
                             self.send_sem[part], self.last[part][way], (own, scene))

        def total(self, part):
            q, slot = self.q, self.slot
            row_a, row_b, row = rows_of(part)
            wait(last.at[q, :, row_a], self.last[part][0])
            wait(last.at[q, :, row_b], self.last[part][1])
            wait(w_out.at[slot, pl.ds(0, n - 1), row], self.send_sem[part])
            out_a, out_b = half[q, y, row_a], half[q, x, row_b]
            for d in range(SIDE - 1):
                out_a, out_b = out_a + last[q, d, row_a], out_b + last[q, d, row_b]
            return jnp.concatenate([out_a, out_b], axis=0)

    class ViewGather:
        def __init__(self, k):
            self.k = k
            self.send_sem, self.rest = [new_sem() for _ in PARTS], [new_sem() for _ in PARTS]
            self.near = [[[new_sem() for _ in range(SIDE - 1)] for _ in range(2)] for _ in PARTS]

        def start(self, part):
            k = self.k
            row_a, row_b, row = rows_of(part, 1)
            z_in[k, view, row] = z_shard[k, row]
            src_a, src_b = z_shard.at[k, row_a], z_shard.at[k, row_b]
            dst_a, dst_b = z_in.at[k, view, row_a], z_in.at[k, view, row_b]
            send_sem, rest = self.send_sem[part], self.rest[part]
            for d in (1, 3, 2):
                push(src_a, dst_a, send_sem, self.near[part][0][d - 1], at_x(d))
                push(src_b, dst_b, send_sem, self.near[part][1][d - 1], at_y(d))
            for d in (1, 3, 2):
                push(src_b, dst_b, send_sem, rest, at_x(d))
                push(src_a, dst_a, send_sem, rest, at_y(d))

        def relay(self, part):
            k = self.k
            row_a, row_b, _ = rows_of(part, 1)
            send_sem, rest = self.send_sem[part], self.rest[part]
            for d in (1, 3, 2):
                from_x, from_y = row_to[SIDE - d], column_to[SIDE - d]
                there_a, there_b = z_in.at[k, from_x, row_a], z_in.at[k, from_y, row_b]
                wait(there_a, self.near[part][0][d - 1])
                for e in (2, 1, 3):
                    push(there_a, there_a, send_sem, rest, at_y(e))
                wait(there_b, self.near[part][1][d - 1])
                for e in (2, 1, 3):
                    push(there_b, there_b, send_sem, rest, at_x(e))

        def finish(self, part):
            k = self.k
            row = rows_of(part, 1)[2]
            wait(z_in.at[k, pl.ds(0, 12), row], self.rest[part])
            wait(z_in.at[k, pl.ds(0, 15), row], self.send_sem[part])
            flat = z_in.at[k].reshape(n * (params + 1) * 8, G)
            first, count = row.start, row.size

            def restage(owner, c):
                for i in range(8):
                    at = owner * (params + 1) * 8 + first * 8 + i
                    z[8 * owner + i, pl.ds(first, count)] = flat[pl.ds(at, count, stride=8), :]
                return c

            lax.fori_loop(0, n, restage, 0, unroll=4)

    colour_row = lax.broadcasted_iota(jnp.int32, (CP, 2 * G), 0) == params - 1
    colour_row = jnp.where(colour_row, 1.0, 0.0).astype(bf16)

    def transpose_rows(left, right_hi, right_lo, tinted):
        lh, ll = split2(left)
        first = dot(jnp.concatenate([lh, ll], axis=0), right_hi, NT)
        tinted = tinted[:, :G] + tinted[:, G:]
        last = dot(colour_row, jnp.concatenate(split2(tinted), axis=1), NT)
        return first[:CP] + first[CP:] + dot(lh, right_lo, NT) + last

    def pair(ref, t):
        return jnp.concatenate([ref[2 * t], ref[2 * t + 1]], axis=0)

    def diagonal(t, c):
        s, w = pair(S, t), pair(W, t)
        put_listing(t, transpose_rows(b16[t] * b16[t], *split2(s * s), w * w))
        return c

    lax.fori_loop(0, tiles, diagonal, 0, unroll=4)
    scatter_blocks(0)
    diag_sum = ViewScatter(0, 0)
    for part in range(2):
        diag_sum.start(part)
    render.publish(render.total())

    def apply_transpose(t, u):
        put_listing(t, transpose_rows(b16[t] * u, pair(hi, t), pair(lo, t), pair(W, t) * u))

    def gradient(t):
        u = lanes(u_now.at[0], 2 * t) - target[pl.ds(t, 1), :]
        residual[pl.ds(t, 1), :] = u
        apply_transpose(t, u)

    half_loop(mine, gradient, 8)
    render.rest()
    half_loop(other, gradient, 8)
    scatter_blocks(1)
    grad_sum = ViewScatter(1, 1)
    for part in range(2):
        grad_sum.start(part)
    for part in range(2):
        diag_sum.middle(part)
    for part in range(2):
        grad_sum.middle(part)

    R, P_, D = 0, 1, 2

    def lane_sum(x):
        return jnp.sum(x, axis=1, keepdims=True)

    def fold(x):
        return jnp.sum(jnp.sum(x, axis=0), axis=0, keepdims=True)

    for part in range(2):
        shard[D, rows_of(part)[2]] = diag_sum.total(part)

    def next_z(k, remainder):
        gather = ViewGather(k)
        inner = [jnp.zeros((1, G), f32)] * 3
        for part in range(2):
            row = rows_of(part)[2]
            r = remainder(part, row)
            shard[R, row] = r
            d = shard[D, row]
            zs = r / ((1.0 + DAMPING) * d + RIDGE)
            dz = (DAMPING * d + RIDGE) * zs
            inner = [inner[0] + fold(r * zs), inner[1] + fold(zs * dz), inner[2] + fold(shard[P_, row] * dz) if k else inner[2]]
            z_shard[k, row] = zs
            if part:
                z_shard[k, params] = jnp.concatenate(inner + [jnp.zeros((5, G), f32)], axis=0)
            gather.start(part)
        gather.relay(0)
        gather.relay(1)
        gather.finish(0)
        gather.finish(1)

    def share_square(k, u):
        squares = rows8(dot_in.at[k], 2 * view + core)
        squares[...] = jnp.broadcast_to(jnp.sum(u * u, axis=0, keepdims=True), (8, G))
        pair_sems = [new_sem(), new_sem()]

        def share(d, c):
            there = lax.rem(view + d, n)
            push(squares, squares, *pair_sems, (there, scene))
            push(squares, squares, *pair_sems, (there, scene + 1 - 2 * core))
            return c

        push(squares, squares, *pair_sems, partner)
        lax.fori_loop(1, n, share, 0)
        return pair_sems

    def all_squares(k, pair_sems):
        wait(dot_in.at[k, pl.ds(0, 8 * (2 * n - 1))], pair_sems[1])
        wait(dot_in.at[k, pl.ds(0, 8 * (2 * n - 1))], pair_sems[0])
        total = dot_in[k, pl.ds(0, 8), :]
        for i in range(1, 2 * n):
            total = total + dot_in[k, pl.ds(8 * i, 8), :]
        return lane_sum(total[0:1])

    one = jnp.ones((1, 1), f32)
    rz_old, pdp = one, 0.0 * one
    remainder = lambda part, row: -grad_sum.total(part)
    for k in range(ITERS):
        next_z(k, remainder)
        tally = z_in[k, 0, params]
        for i in range(1, n):
            tally = tally + z_in[k, i, params]
        tally_out[k] = tally
        tally_sems = [new_sem(), new_sem()]
        rows8(tally_in.at[k], scene)[...] = tally_out[k]
        to_scene(lambda peer: tally_out.at[k], rows8(tally_in.at[k], scene), *tally_sems)

        def forward(t):
            v = jnp.concatenate(
                [z[ids[j, t]] for j in range(2)], axis=1)
            vh, vl = split2(v)
            lhs = jnp.concatenate([vh, vl, vh], axis=0)
            total = jnp.zeros((1, 2 * G), f32)
            for j in range(2):
                p = 2 * t + j
                projected = dot(lhs[:, G * j : G * (j + 1)], bst[t], TN)
                tint = jnp.transpose(v[:, G * j : G * (j + 1)])[:, params - 1 : params]
                total = total + jnp.sum(S[p] * projected + W[p] * tint, axis=0, keepdims=True)
            put_u(t, total)

        product = SceneSum(k + 1)
        product.run(forward, 8)
        wait(some8(tally_in.at[k]), tally_sems[1])
        wait(some8(tally_in.at[k]), tally_sems[0])
        tally = tally_in[k, pl.ds(0, 8), :]
        for i in range(1, n):
            tally = tally + tally_in[k, pl.ds(8 * i, 8), :]
        totals = lane_sum(tally)
        rz, zdz, zdp = totals[0:1], totals[1:2], totals[2:3]
        beta = rz / rz_old if k else 0.0 * one
        u = product.total()
        if k:
            u = u + beta * half_rows(u_now.at[k], mine)[...]
        if k + 1 < ITERS:
            product.publish(u)
        pdp = zdz + 2.0 * beta * zdp + beta * beta * pdp
        pair_sems = share_square(k, u)
        def turn(k=k, beta=beta):
            if k:
                direction[...] = z[...] + beta * direction[...]
                shard[P_] = z_shard[k, pl.ds(0, params)] + beta * shard[P_]
            else:
                direction[...] = z[...]
                shard[P_] = z_shard[k, pl.ds(0, params)]

        if k + 1 < ITERS:
            back = lambda t: apply_transpose(t, lanes(u_now.at[k + 1], 2 * t))
            half_loop(mine, back, 8)
            product.rest()
            half_loop(other, back, 8)
            scatter_blocks(k)
            image_sum = ViewScatter(k + 2, k)
            image_sum.start(0)
            image_sum.start(1)
            turn()
            a = rz / (all_squares(k, pair_sems) + pdp)
            image_sum.middle(0)
            image_sum.middle(1)

            def remainder(part, row, image_sum=image_sum, a=a):
                image = image_sum.total(part) + (DAMPING * shard[D, row] + RIDGE) * shard[P_, row]
                return shard[R, row] - a * image

            if k:
                total_step[...] = total_step[...] + a * direction[...]
            else:
                total_step[...] = a * direction[...]
        else:
            turn()

            def put_step(b, c):
                at = pl.ds(pl.multiple_of(b * G, G), G)
                base[:, at] = total_step[b][:params]
                last_direction[:, at] = direction[b][:params]
                return c

            lax.fori_loop(0, G, put_step, 0, unroll=8)
            a = rz / (all_squares(k, pair_sems) + pdp)
            scale[...] = jnp.broadcast_to(a, scale.shape)
        rz_old = rz


def local(n, params, pixel_basis, tile_blocks, depth_rank, target):
    count = params.shape[0]
    tiles, _, pixels = pixel_basis.shape
    ids = tile_blocks.transpose(1, 2, 0).reshape(2, tiles)
    basis = pixel_basis.transpose(1, 0, 2).reshape((count - 1) * tiles, pixels)
    vmem = pl.BlockSpec(memory_space=pltpu.VMEM)
    lists = 2 * tiles
    base, direction, scale, residual = pl.pallas_call(
        functools.partial(kernel, n, count, tiles),
        out_shape=(
            jax.ShapeDtypeStruct((count, G * G), f32),
            jax.ShapeDtypeStruct((count, G * G), f32),
            jax.ShapeDtypeStruct((1, G * G), f32),
            jax.ShapeDtypeStruct((tiles, pixels), f32),
        ),
        in_specs=[vmem, vmem, pl.BlockSpec(memory_space=pltpu.SMEM), vmem, vmem, vmem],
        out_specs=(vmem,) * 4,
        scratch_shapes=[
            pltpu.VMEM((tiles, CP, pixels), f32),
            pltpu.VMEM((tiles, 3 * CP, pixels), bf16),
            pltpu.VMEM((lists, G, pixels), f32),
            pltpu.VMEM((lists, G, pixels), f32),
            pltpu.VMEM((lists, G, pixels), bf16),
            pltpu.VMEM((lists, G, pixels), bf16),
            pltpu.VMEM((CP * lists, G), f32),
            pltpu.VMEM((G, 2 * lists), bf16),
            pltpu.VMEM((8 * n, G), f32),
            pltpu.VMEM((8 * n, G), f32),
            pltpu.VMEM((8 * n, G), f32),
            pltpu.VMEM((8 * n, G), f32),
            pltpu.VMEM((2 * tiles, G), f32),
            pltpu.VMEM((ITERS + 1, tiles, G), f32),
            pltpu.VMEM((ITERS + 1, n // 2, tiles, G), f32),
            pltpu.VMEM((ITERS + 1, 2 * tiles, G), f32),
            pltpu.VMEM((ITERS, 8, G), f32),
            pltpu.VMEM((ITERS, 8 * n, G), f32),
            pltpu.VMEM((2, n, count, 8, G), f32),
            pltpu.VMEM((ITERS + 1, SIDE - 1, SIDE, count, 8, G), f32),
            pltpu.VMEM((ITERS + 1, SIDE, count, 8, G), f32),
            pltpu.VMEM((ITERS + 1, SIDE - 1, count, 8, G), f32),
            pltpu.VMEM((G, CP, G), f32),
            pltpu.VMEM((ITERS, n, count + 1, 8, G), f32),
            pltpu.VMEM((G, CP, G), f32),
            pltpu.VMEM((G, CP, G), f32),
            pltpu.VMEM((ITERS, count + 1, 8, G), f32),
            pltpu.VMEM((3, count, 8, G), f32),
            pltpu.VMEM((ITERS, 16 * n, G), f32),
            pltpu.SemaphoreType.DMA((SEMS,)),
        ],
        compiler_params=pltpu.CompilerParams(
            collective_id=0, has_side_effects=True, vmem_limit_bytes=64 * 1024 * 1024 - 65536),
        name="lm_step",
    )(params, basis, ids, ids, depth_rank, target)
    return base + scale * direction, residual


def solution(mesh):
    in_specs = (
        P(None, "scene"),
        P("view", None, None),
        P("view", "scene", None),
        P("view", None),
        P("view", None),
    )
    out_specs = (P(None, "scene"), P("view", None))
    step = functools.partial(local, mesh.shape["scene"])
    return jax.shard_map(step, mesh=mesh, in_specs=in_specs, out_specs=out_specs, check_vma=False)
```

```python
import functools

import jax
import jax.numpy as jnp
from jax import lax
from jax.experimental import pallas as pl
from jax.experimental.pallas import tpu as pltpu
from jax.sharding import PartitionSpec as P

MESH = pl.DeviceIdType.MESH
ALPHA = 0.004
DAMPING = 0.1
RIDGE = 0.0001
ITERS = 3
SIDE = 4
SEMS = 224
PARTS = ((0, 4, 8), (8, 11, 14))
G = 128
CP = 16
f32 = jnp.float32
bf16 = jnp.bfloat16
NT = (((1,), (1,)), ((), ()))
TN = (((0,), (0,)), ((), ()))


def split2(x):
    hi = x.astype(bf16)
    return hi, (x - hi.astype(f32)).astype(bf16)


def split3(x):
    hi = x.astype(bf16)
    rest = x - hi.astype(f32)
    mid = rest.astype(bf16)
    return hi, mid, (rest - mid.astype(f32)).astype(bf16)


def dot(a, b, dims=(((1,), (0,)), ((), ()))):
    return lax.dot_general(a, b, dims, preferred_element_type=f32)


def lanes(ref, row):
    return jnp.concatenate([ref[pl.ds(row, 1), :], ref[pl.ds(row + 1, 1), :]], axis=1)


def kernel(
    n, params, tiles,
    par, basis, ids, ids_rows, rank, target,
    base, last_direction, scale, residual,
    b16, bst, S, W, hi, lo, stk, onehot,
    bl_out, bl_in, fr_out, fr_in,
    u_out, u_pair, u_z, u_now, tally_out, tally_in,
    w_out, parts, half, last,
    z, z_in, direction, total_step, z_shard, shard, dot_in,
    sems,
):
    view = lax.axis_index("view")
    scene = lax.axis_index("scene")
    y, x = view // SIDE, lax.rem(view, SIDE)
    zz, core = scene // 2, lax.rem(scene, 2)
    partner = (view, scene + 1 - 2 * core)
    xs = [lax.rem(x + d, SIDE) for d in range(SIDE)]
    ys = [lax.rem(y + d, SIDE) for d in range(SIDE)]
    barrier = pltpu.get_barrier_semaphore()

    def greet(d, c):
        pl.semaphore_signal(barrier, inc=1, device_id=(lax.rem(view + d, n), scene), device_id_type=MESH)
        pl.semaphore_signal(barrier, inc=1, device_id=(lax.rem(view + d, n), scene + 1 - 2 * core), device_id_type=MESH)
        pl.semaphore_signal(barrier, inc=1, device_id=(view, lax.rem(scene + d, n)), device_id_type=MESH)
        return c

    lax.fori_loop(1, n, greet, 0)
    counter = iter(range(SEMS))
    new_sem = lambda: sems.at[next(counter)]

    def push(src, dst, send_sem, recv_sem, where):
        pltpu.make_async_remote_copy(
            src_ref=src, dst_ref=dst, send_sem=send_sem, recv_sem=recv_sem, device_id=where, device_id_type=MESH,
        ).start()

    def wait(ref, sem):
        pltpu.make_async_copy(ref, ref, sem).wait()

    def to_scene(src_of, dst, send_sem, recv_sem):
        def body(d, c):
            peer = lax.rem(scene + d, n)
            push(src_of(peer), dst, send_sem, recv_sem, (view, peer))
            return c

        lax.fori_loop(1, n, body, 0)

    below = lax.broadcasted_iota(jnp.int32, (G, G), 1) < lax.broadcasted_iota(jnp.int32, (G, G), 0)
    below = jnp.where(below, 1.0, 0.0).astype(bf16)
    below = jnp.concatenate([below, below], axis=1)

    halves = [w_out.at[h].reshape(n * params * 8, G) for h in range(2)]
    for h in range(2):
        halves[h][pl.ds(0, (params - 1) * tiles)] = basis[:, G * h : G * (h + 1)]

    def prepare(t, c):
        full = jnp.concatenate([half[pl.ds(t, params - 1, stride=tiles), :] for half in halves], axis=1)
        full = jnp.concatenate([full, jnp.zeros((CP - params + 1, full.shape[1]), f32)], axis=0)
        b16[t] = full
        return c

    lax.fori_loop(0, tiles, prepare, 0, unroll=4)

    def stage(b, c):
        piece = par[:, pl.ds(pl.multiple_of(b * G, G), G)]
        direction[b] = jnp.concatenate([piece, jnp.zeros((CP - params, G), f32)], axis=0)
        return c

    lax.fori_loop(0, G, stage, 0, unroll=8)
    z[:, params + 1 :] = jnp.zeros((G, CP - params - 1, G), f32)

    def listing_params(t, j):
        return direction[ids[j, t]]

    def slot_row(t, j):
        return 8 * (t // 2) + 4 * j + 2 * lax.rem(t, 2)

    def opacities(t, c):
        bh, bm, bl = split3(b16[t])
        rhs = jnp.concatenate([bh, bm, bh, bl, bh, bm], axis=0)
        for j in range(2):
            p = 2 * t + j
            vh, vm, vl = split3(listing_params(t, j))
            lhs = jnp.concatenate([vh, vh, vm, vh, vl, vm], axis=0)
            logit = dot(lhs, rhs, TN)
            o = 0.5 * ALPHA + 0.5 * ALPHA * jnp.tanh(0.5 * logit)
            keep = -o * (1.0 + o * (0.5 + o * (1.0 / 3.0 + o * 0.25)))
            W[p] = o
            kh, kl = split2(keep)
            hi[p] = kh
            lo[p] = kl
            total = jnp.sum(keep, axis=0, keepdims=True)
            r = slot_row(t, j)
            bl_out[pl.ds(r, 1), :] = total[:, :G]
            bl_out[pl.ds(r + 1, 1), :] = total[:, G:]
        return c

    lax.fori_loop(0, tiles, opacities, 0, unroll=8)

    pl.semaphore_wait(barrier, 3 * (n - 1))
    rows8 = lambda ref, i: ref.at[pl.ds(pl.multiple_of(i * 8, 8), 8)]
    some8 = lambda ref: ref.at[pl.ds(0, 8 * (n - 1))]
    front_sems = [new_sem() for _ in range(4)]
    to_scene(lambda peer: rows8(bl_out, peer), rows8(bl_in, scene), front_sems[0], front_sems[1])
    rows8(bl_in, scene)[...] = rows8(bl_out, scene)[...]

    block_at = lax.broadcasted_iota(jnp.int32, (G, tiles), 0)
    hot = [jnp.where(block_at == ids_rows[pl.ds(j, 1), :], 1.0, 0.0).astype(bf16) for j in range(2)]
    onehot[...] = jnp.concatenate(hot + hot, axis=1)

    def basis_halves(t, c):
        bh, bl = split2(b16[t])
        bst[t] = jnp.concatenate([bh, bh, bl], axis=0)
        return c

    lax.fori_loop(0, tiles, basis_halves, 0, unroll=4)

    def weights(t, c):
        for j in range(2):
            p = 2 * t + j
            keeps = jnp.concatenate([hi[p], lo[p]], axis=0)
            inner = dot(below, keeps)
            o = W[p]
            colour = jnp.transpose(listing_params(t, j))[:, params - 1 : params]
            w = jnp.exp(inner) * o
            W[p] = w
            S[p] = w * colour * (1.0 - o * (1.0 / ALPHA))
        return c

    lax.fori_loop(0, tiles // 4, weights, 0, unroll=8)

    wait(some8(bl_in), front_sems[1])
    wait(some8(bl_out), front_sems[0])
    slots = 2 * n
    eye = lax.broadcasted_iota(jnp.int32, (slots, slots), 0) == lax.broadcasted_iota(jnp.int32, (slots, slots), 1)
    for i in range(2):
        rank_row = jnp.broadcast_to(rank[pl.ds(2 * scene + i, 1), :].astype(f32), (slots, slots))
        rank_col = jnp.sum(jnp.where(eye, rank_row, 0.0), axis=1, keepdims=True)
        earlier = jnp.where(rank_row < rank_col, 1.0, 0.0).astype(bf16)
        for h in range(2):
            lh, lm, ll = split3(bl_in[pl.ds(2 * i + h, slots, stride=4), :])
            front = dot(earlier, lh) + dot(earlier, lm) + dot(earlier, ll)
            fr_out[pl.ds(2 * i + h, slots, stride=4), :] = jnp.exp(front)
    to_scene(lambda peer: rows8(fr_out, peer), rows8(fr_in, scene), front_sems[2], front_sems[3])
    rows8(fr_in, scene)[...] = rows8(fr_out, scene)[...]

    lax.fori_loop(tiles // 4, tiles, weights, 0, unroll=8)
    wait(some8(fr_in), front_sems[3])
    wait(some8(fr_out), front_sems[2])

    def put_u(t, value):
        u_out[pl.ds(2 * t, 1), :] = value[:, :G]
        u_out[pl.ds(2 * t + 1, 1), :] = value[:, G:]

    mine, other = core * (tiles // 2), (1 - core) * (tiles // 2)

    def half_loop(first, body, unroll):
        def step_of(i, c):
            body(first + i)
            return c

        lax.fori_loop(0, tiles // 2, step_of, 0, unroll=unroll)

    def finish(t):
        total = jnp.zeros((1, 2 * G), f32)
        for j in range(2):
            p = 2 * t + j
            factor = lanes(fr_in, slot_row(t, j))
            w = W[p] * factor
            s = S[p] * factor
            W[p] = w
            S[p] = s
            hi[p], lo[p] = split2(s)
            colour = jnp.transpose(listing_params(t, j))[:, params - 1 : params]
            total = total + jnp.sum(w * colour, axis=0, keepdims=True)
        put_u(t, total)

    def rows_of(part, more=0):
        a, b, end = PARTS[part]
        end = end + more * part
        return pl.ds(a, b - a), pl.ds(b, end - b), pl.ds(a, end - a)

    row_to = [y * SIDE + xs[d] for d in range(SIDE)]
    column_to = [ys[d] * SIDE + x for d in range(SIDE)]
    at_x = lambda d: (row_to[d], scene)
    at_y = lambda d: (column_to[d], scene)

    half_rows = lambda ref, first: ref.at[pl.ds(pl.multiple_of(2 * first, 8), tiles)]

    class SceneSum:
        def __init__(self, q):
            self.q, self.sems = q, [new_sem() for _ in range(7)]

        def run(self, body, unroll):
            q, sem = self.q, self.sems
            quarter = tiles // 4

            def part_loop(first):
                def step_of(i, c):
                    body(first + i)
                    return c

                lax.fori_loop(0, quarter, step_of, 0, unroll=unroll)

            rows = lambda ref, first: ref.at[pl.ds(pl.multiple_of(2 * first, 8), 2 * quarter)]
            for i in range(2):
                part_loop(other + i * quarter)
                push(rows(u_out, other + i * quarter), rows(u_pair.at[q], i * quarter), sem[0], sem[1 + 5 * i], partner)
            for i in range(2):
                part_loop(mine + i * quarter)
                pair_rows, z_rows = rows(u_pair.at[q], i * quarter), rows(u_z.at[q, zz], i * quarter)
                wait(pair_rows, sem[1 + 5 * i])
                z_rows[...] = rows(u_out, mine + i * quarter)[...] + pair_rows[...]
                for d in (4, 3, 5, 2, 6, 1, 7):
                    push(z_rows, z_rows, sem[2], sem[3], (view, lax.rem(scene + 2 * d, n)))
            wait(u_pair.at[q], sem[0])

        def total(self):
            q, sem = self.q, self.sems
            wait(u_z.at[q, pl.ds(0, n // 2 - 1)], sem[3])
            wait(u_z.at[q, pl.ds(0, n // 2 - 1)], sem[2])
            out = u_z[q, 0]
            for i in range(1, n // 2):
                out = out + u_z[q, i]
            return out

        def publish(self, value):
            q, sem = self.q, self.sems
            rows = half_rows(u_now.at[q], mine)
            rows[...] = value
            push(rows, rows, sem[4], sem[5], partner)

        def rest(self):
            q, sem = self.q, self.sems
            wait(half_rows(u_now.at[q], other), sem[5])
            wait(half_rows(u_now.at[q], other), sem[4])

    render = SceneSum(0)
    render.run(finish, 2)

    def scatter_blocks(slot):
        for c in range(0, params, 2):
            x = jnp.concatenate([stk[pl.ds((c + e) * 2 * tiles, 2 * tiles), :] for e in range(2)], axis=1)
            xh, xl = split2(x)
            out = dot(onehot[...], jnp.concatenate([xh, xl], axis=0))
            w_out[slot, :, c] = out[:, :G].reshape(n, 8, G)
            w_out[slot, :, c + 1] = out[:, G:].reshape(n, 8, G)

    def put_listing(t, value):
        for j in range(2):
            stk[pl.ds(tiles * j + t, CP, stride=2 * tiles), :] = value[:, G * j : G * (j + 1)]

    class ViewScatter:
        def __init__(self, q, slot):
            self.q, self.slot = q, slot
            self.send_sem = [new_sem() for _ in PARTS]
            self.last = [[new_sem(), new_sem()] for _ in PARTS]
            self.first = [[[new_sem() for _ in range(SIDE)] for _ in range(2)] for _ in PARTS]

        def start(self, part):
            q, slot = self.q, self.slot
            row_a, row_b, _ = rows_of(part)
            for e in (2, 1, 3, 0):
                for d in (2, 1, 3):
                    to_x, to_y, line_y, line_x = xs[d], ys[d], ys[e], xs[e]
                    push(w_out.at[slot, line_y * SIDE + to_x, row_a], parts.at[q, d - 1, line_y, row_a],
                         self.send_sem[part], self.first[part][0][e], at_x(d))
                    push(w_out.at[slot, to_y * SIDE + line_x, row_b], parts.at[q, d - 1, line_x, row_b],
                         self.send_sem[part], self.first[part][1][e], at_y(d))

        def middle(self, part):
            q, slot = self.q, self.slot
            row_a, row_b, _ = rows_of(part)
            for e in (2, 1, 3, 0):
                for own, line, row, way in ((column_to[e], ys[e], row_a, 0), (row_to[e], xs[e], row_b, 1)):
                    wait(parts.at[q, :, line, row], self.first[part][way][e])
                    total = w_out[slot, own, row] + parts[q, 0, line, row]
                    half[q, line, row] = total + parts[q, 1, line, row] + parts[q, 2, line, row]
                    if e:
                        push(half.at[q, line, row], last.at[q, e - 1, row],
                             self.send_sem[part], self.last[part][way], (own, scene))

        def total(self, part):
            q, slot = self.q, self.slot
            row_a, row_b, row = rows_of(part)
            wait(last.at[q, :, row_a], self.last[part][0])
            wait(last.at[q, :, row_b], self.last[part][1])
            wait(w_out.at[slot, pl.ds(0, n - 1), row], self.send_sem[part])
            out_a, out_b = half[q, y, row_a], half[q, x, row_b]
            for d in range(SIDE - 1):
                out_a, out_b = out_a + last[q, d, row_a], out_b + last[q, d, row_b]
            return jnp.concatenate([out_a, out_b], axis=0)

    class ViewGather:
        def __init__(self, k):
            self.k = k
            self.send_sem, self.rest = [new_sem() for _ in PARTS], [new_sem() for _ in PARTS]
            self.near = [[[new_sem() for _ in range(SIDE - 1)] for _ in range(2)] for _ in PARTS]

        def start(self, part):
            k = self.k
            row_a, row_b, row = rows_of(part, 1)
            z_in[k, view, row] = z_shard[k, row]
            src_a, src_b = z_shard.at[k, row_a], z_shard.at[k, row_b]
            dst_a, dst_b = z_in.at[k, view, row_a], z_in.at[k, view, row_b]
            send_sem, rest = self.send_sem[part], self.rest[part]
            for d in (1, 3, 2):
                push(src_a, dst_a, send_sem, self.near[part][0][d - 1], at_x(d))
                push(src_b, dst_b, send_sem, self.near[part][1][d - 1], at_y(d))
            for d in (1, 3, 2):
                push(src_b, dst_b, send_sem, rest, at_x(d))
                push(src_a, dst_a, send_sem, rest, at_y(d))

        def relay(self, part):
            k = self.k
            row_a, row_b, _ = rows_of(part, 1)
            send_sem, rest = self.send_sem[part], self.rest[part]
            for d in (1, 3, 2):
                from_x, from_y = row_to[SIDE - d], column_to[SIDE - d]
                there_a, there_b = z_in.at[k, from_x, row_a], z_in.at[k, from_y, row_b]
                wait(there_a, self.near[part][0][d - 1])
                for e in (2, 1, 3):
                    push(there_a, there_a, send_sem, rest, at_y(e))
                wait(there_b, self.near[part][1][d - 1])
                for e in (2, 1, 3):
                    push(there_b, there_b, send_sem, rest, at_x(e))

        def finish(self, part):
            k = self.k
            row = rows_of(part, 1)[2]
            wait(z_in.at[k, pl.ds(0, 12), row], self.rest[part])
            wait(z_in.at[k, pl.ds(0, 15), row], self.send_sem[part])
            flat = z_in.at[k].reshape(n * (params + 1) * 8, G)
            first, count = row.start, row.size

            def restage(owner, c):
                for i in range(8):
                    at = owner * (params + 1) * 8 + first * 8 + i
                    z[8 * owner + i, pl.ds(first, count)] = flat[pl.ds(at, count, stride=8), :]
                return c

            lax.fori_loop(0, n, restage, 0, unroll=4)

    colour_row = lax.broadcasted_iota(jnp.int32, (CP, 2 * G), 0) == params - 1
    colour_row = jnp.where(colour_row, 1.0, 0.0).astype(bf16)

    def transpose_rows(left, right_hi, right_lo, tinted):
        lh, ll = split2(left)
        first = dot(jnp.concatenate([lh, ll], axis=0), right_hi, NT)
        tinted = tinted[:, :G] + tinted[:, G:]
        last = dot(colour_row, jnp.concatenate(split2(tinted), axis=1), NT)
        return first[:CP] + first[CP:] + dot(lh, right_lo, NT) + last

    def pair(ref, t):
        return jnp.concatenate([ref[2 * t], ref[2 * t + 1]], axis=0)

    def diagonal(t, c):
        s, w = pair(S, t), pair(W, t)
        put_listing(t, transpose_rows(b16[t] * b16[t], *split2(s * s), w * w))
        return c

    lax.fori_loop(0, tiles, diagonal, 0, unroll=4)
    scatter_blocks(0)
    diag_sum = ViewScatter(0, 0)
    for part in range(2):
        diag_sum.start(part)
    render.publish(render.total())

    def apply_transpose(t, u):
        put_listing(t, transpose_rows(b16[t] * u, pair(hi, t), pair(lo, t), pair(W, t) * u))

    def gradient(t):
        u = lanes(u_now.at[0], 2 * t) - target[pl.ds(t, 1), :]
        residual[pl.ds(t, 1), :] = u
        apply_transpose(t, u)

    half_loop(mine, gradient, 8)
    render.rest()
    half_loop(other, gradient, 8)
    scatter_blocks(1)
    grad_sum = ViewScatter(1, 1)
    for part in range(2):
        grad_sum.start(part)
    for part in range(2):
        diag_sum.middle(part)
    for part in range(2):
        grad_sum.middle(part)

    R, P_, D = 0, 1, 2

    def lane_sum(x):
        return jnp.sum(x, axis=1, keepdims=True)

    def fold(x):
        return jnp.sum(jnp.sum(x, axis=0), axis=0, keepdims=True)

    for part in range(2):
        shard[D, rows_of(part)[2]] = diag_sum.total(part)

    def next_z(k, remainder):
        gather = ViewGather(k)
        inner = [jnp.zeros((1, G), f32)] * 3
        for part in range(2):
            row = rows_of(part)[2]
            r = remainder(part, row)
            shard[R, row] = r
            d = shard[D, row]
            zs = r / ((1.0 + DAMPING) * d + RIDGE)
            dz = (DAMPING * d + RIDGE) * zs
            inner = [inner[0] + fold(r * zs), inner[1] + fold(zs * dz), inner[2] + fold(shard[P_, row] * dz) if k else inner[2]]
            z_shard[k, row] = zs
            if part:
                z_shard[k, params] = jnp.concatenate(inner + [jnp.zeros((5, G), f32)], axis=0)
            gather.start(part)
        gather.relay(0)
        gather.relay(1)
        gather.finish(0)
        gather.finish(1)

    def share_square(k, u):
        squares = rows8(dot_in.at[k], 2 * view + core)
        squares[...] = jnp.broadcast_to(jnp.sum(u * u, axis=0, keepdims=True), (8, G))
        pair_sems = [new_sem(), new_sem()]

        def share(d, c):
            there = lax.rem(view + d, n)
            push(squares, squares, *pair_sems, (there, scene))
            push(squares, squares, *pair_sems, (there, scene + 1 - 2 * core))
            return c

        push(squares, squares, *pair_sems, partner)
        lax.fori_loop(1, n, share, 0)
        return pair_sems

    def all_squares(k, pair_sems):
        wait(dot_in.at[k, pl.ds(0, 8 * (2 * n - 1))], pair_sems[1])
        wait(dot_in.at[k, pl.ds(0, 8 * (2 * n - 1))], pair_sems[0])
        total = dot_in[k, pl.ds(0, 8), :]
        for i in range(1, 2 * n):
            total = total + dot_in[k, pl.ds(8 * i, 8), :]
        return lane_sum(total[0:1])

    one = jnp.ones((1, 1), f32)
    rz_old, pdp = one, 0.0 * one
    remainder = lambda part, row: -grad_sum.total(part)
    for k in range(ITERS):
        next_z(k, remainder)
        tally = z_in[k, 0, params]
        for i in range(1, n):
            tally = tally + z_in[k, i, params]
        tally_out[k] = tally
        tally_sems = [new_sem(), new_sem()]
        rows8(tally_in.at[k], scene)[...] = tally_out[k]
        to_scene(lambda peer: tally_out.at[k], rows8(tally_in.at[k], scene), *tally_sems)

        def forward(t):
            v = jnp.concatenate(
                [z[ids[j, t]] for j in range(2)], axis=1)
            vh, vl = split2(v)
            lhs = jnp.concatenate([vh, vl, vh], axis=0)
            total = jnp.zeros((1, 2 * G), f32)
            for j in range(2):
                p = 2 * t + j
                projected = dot(lhs[:, G * j : G * (j + 1)], bst[t], TN)
                tint = jnp.transpose(v[:, G * j : G * (j + 1)])[:, params - 1 : params]
                total = total + jnp.sum(S[p] * projected + W[p] * tint, axis=0, keepdims=True)
            put_u(t, total)

        product = SceneSum(k + 1)
        product.run(forward, 8)
        wait(some8(tally_in.at[k]), tally_sems[1])
        wait(some8(tally_in.at[k]), tally_sems[0])
        tally = tally_in[k, pl.ds(0, 8), :]
        for i in range(1, n):
            tally = tally + tally_in[k, pl.ds(8 * i, 8), :]
        totals = lane_sum(tally)
        rz, zdz, zdp = totals[0:1], totals[1:2], totals[2:3]
        beta = rz / rz_old if k else 0.0 * one
        u = product.total()
        if k:
            u = u + beta * half_rows(u_now.at[k], mine)[...]
        if k + 1 < ITERS:
            product.publish(u)
        pdp = zdz + 2.0 * beta * zdp + beta * beta * pdp
        pair_sems = share_square(k, u)
        def turn(k=k, beta=beta):
            if k:
                direction[...] = z[...] + beta * direction[...]
                shard[P_] = z_shard[k, pl.ds(0, params)] + beta * shard[P_]
            else:
                direction[...] = z[...]
                shard[P_] = z_shard[k, pl.ds(0, params)]

        if k + 1 < ITERS:
            back = lambda t: apply_transpose(t, lanes(u_now.at[k + 1], 2 * t))
            half_loop(mine, back, 8)
            product.rest()
            half_loop(other, back, 8)
            scatter_blocks(k)
            image_sum = ViewScatter(k + 2, k)
            image_sum.start(0)
            image_sum.start(1)
            turn()
            a = rz / (all_squares(k, pair_sems) + pdp)
            image_sum.middle(0)
            image_sum.middle(1)

            def remainder(part, row, image_sum=image_sum, a=a):
                image = image_sum.total(part) + (DAMPING * shard[D, row] + RIDGE) * shard[P_, row]
                return shard[R, row] - a * image

            if k:
                total_step[...] = total_step[...] + a * direction[...]
            else:
                total_step[...] = a * direction[...]
        else:
            turn()

            def put_step(b, c):
                at = pl.ds(pl.multiple_of(b * G, G), G)
                base[:, at] = total_step[b][:params]
                last_direction[:, at] = direction[b][:params]
                return c

            lax.fori_loop(0, G, put_step, 0, unroll=8)
            a = rz / (all_squares(k, pair_sems) + pdp)
            scale[...] = jnp.broadcast_to(a, scale.shape)
        rz_old = rz


def local(n, params, pixel_basis, tile_blocks, depth_rank, target):
    count = params.shape[0]
    tiles, _, pixels = pixel_basis.shape
    ids = tile_blocks.transpose(1, 2, 0).reshape(2, tiles)
    basis = pixel_basis.transpose(1, 0, 2).reshape((count - 1) * tiles, pixels)
    vmem = pl.BlockSpec(memory_space=pltpu.VMEM)
    lists = 2 * tiles
    base, direction, scale, residual = pl.pallas_call(
        functools.partial(kernel, n, count, tiles),
        out_shape=(
            jax.ShapeDtypeStruct((count, G * G), f32),
            jax.ShapeDtypeStruct((count, G * G), f32),
            jax.ShapeDtypeStruct((1, G * G), f32),
            jax.ShapeDtypeStruct((tiles, pixels), f32),
        ),
        in_specs=[vmem, vmem, pl.BlockSpec(memory_space=pltpu.SMEM), vmem, vmem, vmem],
        out_specs=(vmem,) * 4,
        scratch_shapes=[
            pltpu.VMEM((tiles, CP, pixels), f32),
            pltpu.VMEM((tiles, 3 * CP, pixels), bf16),
            pltpu.VMEM((lists, G, pixels), f32),
            pltpu.VMEM((lists, G, pixels), f32),
            pltpu.VMEM((lists, G, pixels), bf16),
            pltpu.VMEM((lists, G, pixels), bf16),
            pltpu.VMEM((CP * lists, G), f32),
            pltpu.VMEM((G, 2 * lists), bf16),
            pltpu.VMEM((8 * n, G), f32),
            pltpu.VMEM((8 * n, G), f32),
            pltpu.VMEM((8 * n, G), f32),
            pltpu.VMEM((8 * n, G), f32),
            pltpu.VMEM((2 * tiles, G), f32),
            pltpu.VMEM((ITERS + 1, tiles, G), f32),
            pltpu.VMEM((ITERS + 1, n // 2, tiles, G), f32),
            pltpu.VMEM((ITERS + 1, 2 * tiles, G), f32),
            pltpu.VMEM((ITERS, 8, G), f32),
            pltpu.VMEM((ITERS, 8 * n, G), f32),
            pltpu.VMEM((2, n, count, 8, G), f32),
            pltpu.VMEM((ITERS + 1, SIDE - 1, SIDE, count, 8, G), f32),
            pltpu.VMEM((ITERS + 1, SIDE, count, 8, G), f32),
            pltpu.VMEM((ITERS + 1, SIDE - 1, count, 8, G), f32),
            pltpu.VMEM((G, CP, G), f32),
            pltpu.VMEM((ITERS, n, count + 1, 8, G), f32),
            pltpu.VMEM((G, CP, G), f32),
            pltpu.VMEM((G, CP, G), f32),
            pltpu.VMEM((ITERS, count + 1, 8, G), f32),
            pltpu.VMEM((3, count, 8, G), f32),
            pltpu.VMEM((ITERS, 16 * n, G), f32),
            pltpu.SemaphoreType.DMA((SEMS,)),
        ],
        compiler_params=pltpu.CompilerParams(
            collective_id=0, has_side_effects=True, vmem_limit_bytes=64 * 1024 * 1024 - 65536),
        name="lm_step",
    )(params, basis, ids, ids, depth_rank, target)
    return base + scale * direction, residual


def solution(mesh):
    in_specs = (
        P(None, "scene"),
        P("view", None, None),
        P("view", "scene", None),
        P("view", None),
        P("view", None),
    )
    out_specs = (P(None, "scene"), P("view", None))
    step = functools.partial(local, mesh.shape["scene"])
    return jax.shard_map(step, mesh=mesh, in_specs=in_specs, out_specs=out_specs, check_vma=False)
```
